768 devices in a mesh: loop: 24 (over z_lo, x), grp: 32 (over z_hi, y, core).
Axes of the slice: x: 4, y: 8, z: 12 (z_hi: 2, z_lo: 6; z = z_hi * 6 + z_lo), core: 2. Of those that a mesh axis runs over, the one named last changes fastest.
Arguments:
- queries: bfloat16 [12288, 1024], P(('loop', 'grp')), may hold values from -100 to 100
- landmarks: bfloat16 [49152, 1024], P(('loop', 'grp')), may hold values from -20 to 20
- labels: bfloat16 [49152, 128], P(('loop', 'grp')), may hold values from -6 to 6
- tile_mask: int32 [24, 768], replicated, may hold values from 0 to 1, as said below
Outputs:
- label_scores: bfloat16 [12288, 128], P(('loop', 'grp'))
The draws below stay inside these ranges and needn't reach their ends.
Inputs may be any that keep to these rules, and one draw needn't show every extreme that they name: `tile_mask`: every query tile lists at least one landmark tile.
All inputs are finite; a program needn't handle non-finite values.
Results may differ from the reference program's by a relative error of at most 0.0065.
Values may be sent and summed in bfloat16 or wider, within the bound.
No kernel may reach another device: no remote copies, remote signals or barrier semaphores. Data moves between devices by JAX's collectives and lax.ppermute only.
A program may use at most 32 MiB of HBM per device.

```python
import math
import jax
import jax.numpy as jnp
from jax import lax

D = 1024
C = 128
LDEV = 64
Q_TILE = 512
Q_TILES = 24
QUERIES = 12288
L_TILES = 768
LANDMARKS = 49152


def tile_lists(key):
    base_key = jax.random.fold_in(key, 11)
    key_rate = jax.random.fold_in(base_key, 1)
    key_bits = jax.random.fold_in(base_key, 2)
    key_pick = jax.random.fold_in(base_key, 3)
    threshold = jax.random.randint(key_rate, (Q_TILES, 1), 2, 33)
    draw_bits = jax.random.randint(key_bits, (Q_TILES, L_TILES), 0, 64)
    forced = jax.random.randint(key_pick, (Q_TILES,), 0, L_TILES)
    tile_ids = jnp.arange(L_TILES, dtype=jnp.int32)
    listed = (draw_bits < threshold) | (tile_ids[None, :] == forced[:, None])
    return (listed.astype(jnp.int32), forced)


def tile_strength(tile_ids):
    phase = tile_ids % 3
    target = jnp.where(phase == 0, 220.0, jnp.where(phase == 1, 320.0, 420.0)).astype(jnp.float32)
    return 0.5 + target / (4.0 * math.sqrt(D))


def landmark_rows(key):
    land_key = jax.random.fold_in(key, 31)
    values = jnp.clip(jax.random.normal(land_key, (LANDMARKS, D), jnp.float32), -6.0, 6.0)
    tile_ids = jnp.arange(L_TILES, dtype=jnp.int32)
    strength = tile_strength(tile_ids)
    stretch = 2.0 / (4.0 * math.sqrt(D) * (strength - 1.0))
    first_rows = values[tile_ids * LDEV]
    values = values.at[tile_ids * LDEV + 1].set(first_rows * (1.0 + stretch)[:, None])
    return values


def draw_tile_mask(key, part):
    listed, forced = tile_lists(key)
    return listed


def draw_landmarks(key, part):
    return landmark_rows(key).astype(jnp.bfloat16)


def draw_queries(key, part):
    query_key = jax.random.fold_in(key, 21)
    values = jnp.clip(jax.random.normal(query_key, (QUERIES, D), jnp.float32), -6.0, 6.0)
    listed, forced = tile_lists(key)
    land_values = landmark_rows(key).astype(jnp.bfloat16).astype(jnp.float32)
    strength = tile_strength(forced)
    targets = land_values[forced * LDEV] * strength[:, None]
    values = values.at[jnp.arange(Q_TILES, dtype=jnp.int32) * Q_TILE].set(targets)
    return values.astype(jnp.bfloat16)


def levels(key, extent, pieces, least, high):
    factor_of, own = 1.0, jax.random.fold_in(key, 6)
    for dim, shards_of in pieces:
        draws = jnp.exp(jax.random.uniform(jax.random.fold_in(own, dim), (shards_of,), jnp.float32, least / len(pieces), high / len(pieces)))
        factor_of = factor_of * jnp.repeat(draws, extent[dim] // shards_of).reshape([-1 if axis == dim else 1 for axis in range(len(extent))])
    return factor_of


def scatter_about(own_key, shape, deviation, limit, cuts=(), held_as=jnp.bfloat16):
    result = jax.random.normal(own_key, shape, jnp.float32) * deviation
    if len(cuts) > 0:
        result = levels(own_key, shape, cuts, -0.22, 0.18) * result
    return jnp.clip(result, min=-limit, max=limit).astype(held_as)


def setup_inputs(seed: int = 0) -> dict:
    key_of = jax.random.split(jax.random.key(seed), 5)
    return {
        "queries": draw_queries(jax.random.fold_in(key_of[4], 71), 0),
        "landmarks": draw_landmarks(jax.random.fold_in(key_of[4], 71), 0),
        "labels": scatter_about(key_of[2], (LANDMARKS, C), 1.0, 6.0, ((0, 768),)),
        "tile_mask": draw_tile_mask(jax.random.fold_in(key_of[4], 71), 0),
    }


def reference(queries, landmarks, labels, tile_mask):
    scale_factor = 4.0 / math.sqrt(D)
    land_f = landmarks.astype(jnp.float32)
    half_norm = 0.5 * lax.optimization_barrier(jnp.sum(land_f * land_f, axis=1))
    listed = jnp.repeat(tile_mask, LDEV, axis=1) > 0
    query_tiles = queries.reshape(Q_TILES, Q_TILE, D)

    def per_tile(tile_args):
        query_slab, listed_row = tile_args
        logits = lax.dot_general(query_slab, landmarks, (((1,), (1,)), ((), ())), preferred_element_type=jnp.float32)
        logits = (logits - half_norm[None, :]) * scale_factor
        masked = jnp.where(listed_row[None, :], logits, jnp.float32(-1e+30))
        row_max = lax.optimization_barrier(jnp.max(masked, axis=1, keepdims=True))
        kernel = jnp.where(listed_row[None, :], jnp.exp(logits - row_max), jnp.float32(0.0))
        weight_sum = lax.optimization_barrier(jnp.sum(kernel, axis=1))
        label_sum = jnp.dot(kernel.astype(jnp.bfloat16), labels, preferred_element_type=jnp.float32)
        return (label_sum / weight_sum[:, None]).astype(jnp.bfloat16)
    scores_out = lax.map(per_tile, (query_tiles, listed))
    return scores_out.reshape(QUERIES, C)
```

```python
import math

import jax
import jax.numpy as jnp
from jax import lax
from jax.experimental import pallas as pl
from jax.experimental.pallas import tpu as pltpu
from jax.sharding import Mesh, PartitionSpec as P

ZL, X, ZH, Y, CORE = 6, 4, 2, 8, 2
NAMES = ("zl", "x", "zh", "y", "c")
Q_AXES = ("x", "zl", "zh")
SOURCES = X * ZL * ZH
UNLISTED = -1e30


def gather_direct(value, axes, count):
    copies = jnp.broadcast_to(value[None], (count,) + value.shape)
    return lax.all_to_all(copies, axes, 0, 0, tiled=True)


def split3(value):
    high = value.astype(jnp.bfloat16)
    rest = value - high.astype(jnp.float32)
    middle = rest.astype(jnp.bfloat16)
    low = (rest - middle.astype(jnp.float32)).astype(jnp.bfloat16)
    return high, middle, low


def score_kernel(queries_ref, land_ref, bias_ref, out_ref, *, width, chunk, tile_rows, scale):
    rows = queries_ref.shape[0]
    lands = land_ref.shape[0]
    tiles = chunk // tile_rows

    def step(index):
        start = pl.multiple_of(index * chunk, chunk)
        logits = lax.dot_general(
            queries_ref[pl.ds(start, chunk), :],
            land_ref[:, :width],
            (((1,), (1,)), ((), ())),
            preferred_element_type=jnp.float32,
        )
        bias = bias_ref[index]
        logits = (logits * scale).reshape(tiles, tile_rows, lands) + bias[:, None, :]
        logits = logits.reshape(chunk, lands)
        row_max = jnp.max(logits, axis=1, keepdims=True)
        kernel = jnp.exp(logits - row_max)
        weight_sum = jnp.sum(kernel, axis=1, keepdims=True)
        label_sum = jnp.dot(
            kernel.astype(jnp.bfloat16), land_ref[:, width:], preferred_element_type=jnp.float32
        )
        out_ref[pl.ds(start, chunk), :128] = (label_sum / weight_sum).astype(jnp.bfloat16)
        lane = lax.broadcasted_iota(jnp.int32, (chunk, 128), 1)
        stats = jnp.zeros((chunk, 128), jnp.float32)
        for place, piece in enumerate(split3(row_max) + split3(weight_sum)):
            stats = jnp.where(lane == place, piece.astype(jnp.float32), stats)
        out_ref[pl.ds(start, chunk), 128:] = stats.astype(jnp.bfloat16)

    pl.loop(0, rows // chunk)(step)


def score(queries, land, bias, width, tile_rows, scale):
    rows = queries.shape[0]
    lands = land.shape[0]
    classes = land.shape[1] - width
    chunk = 8 * tile_rows
    kernel = lambda *refs: score_kernel(
        *refs, width=width, chunk=chunk, tile_rows=tile_rows, scale=scale
    )
    return pl.pallas_call(
        kernel,
        out_shape=jax.ShapeDtypeStruct((rows, classes + 128), jnp.bfloat16),
        in_specs=[pl.BlockSpec(memory_space=pltpu.VMEM)] * 3,
        out_specs=pl.BlockSpec(memory_space=pltpu.VMEM),
        cost_estimate=pl.CostEstimate(
            flops=2 * rows * lands * (width + classes),
            bytes_accessed=2 * (rows * width + lands * (width + classes) + rows * 256),
            transcendentals=rows * lands,
        ),
        name="score",
    )(queries, land, bias.reshape(rows // chunk, 8, lands))


def merge_kernel(parts_ref, out_ref):
    stats = parts_ref[:, :, 128:].astype(jnp.float32)
    row_max = stats[:, :, 0:1] + stats[:, :, 1:2] + stats[:, :, 2:3]
    weight = stats[:, :, 3:4] + stats[:, :, 4:5] + stats[:, :, 5:6]
    joint = jnp.max(row_max, axis=0, keepdims=True)
    weight = weight * jnp.exp(row_max - joint)
    total = jnp.sum(weight, axis=0)
    labels = jnp.sum(parts_ref[:, :, :128].astype(jnp.float32) * weight, axis=0)
    out_ref[...] = (labels / total).astype(jnp.bfloat16)


def local(queries, landmarks, labels, tile_mask):
    rows, width = queries.shape
    tile_lands, classes = labels.shape
    scale = 4.0 / math.sqrt(width)
    packed = jnp.concatenate([landmarks, labels], axis=1)
    own = gather_direct(packed, "y", Y).reshape(Y * tile_lands, width + classes)
    other = lax.ppermute(own, "c", [(0, 1), (1, 0)])
    land = jnp.concatenate([own, other], axis=0)

    gathered = gather_direct(queries, ("zl", "zh"), ZL * ZH).reshape(ZL * ZH * rows, width)
    gathered = gather_direct(gathered, "x", X).reshape(SOURCES * rows, width)

    place = lax.axis_index("zl") * X + lax.axis_index("x")
    first = (place * ZH + lax.axis_index("zh")) * (Y * CORE)
    listed = lax.dynamic_slice_in_dim(tile_mask, first, Y * CORE, 1)
    listed = listed.reshape(ZL, X, Y, CORE).transpose(1, 0, 3, 2)
    listed = jnp.where(lax.axis_index("c") == 0, listed, listed[:, :, ::-1])
    listed = listed.reshape(X * ZL, CORE * Y) > 0
    land_f = land[:, :width].astype(jnp.float32)
    half_norm = 0.5 * jnp.sum(land_f * land_f, axis=1)
    bias = jnp.where(
        jnp.repeat(listed, tile_lands, axis=1), -scale * half_norm[None, :], jnp.float32(UNLISTED)
    )

    parts = score(gathered, land, bias, width, ZH * rows, scale)
    parts = lax.all_to_all(parts.reshape(SOURCES, rows, classes + 128), Q_AXES, 0, 0, tiled=True)
    return pl.pallas_call(
        merge_kernel,
        out_shape=jax.ShapeDtypeStruct((rows, classes), jnp.bfloat16),
        in_specs=[pl.BlockSpec(memory_space=pltpu.VMEM)],
        out_specs=pl.BlockSpec(memory_space=pltpu.VMEM),
        name="merge",
    )(parts)


def solution(mesh):
    physical = Mesh(mesh.devices.reshape(ZL, X, ZH, Y, CORE), NAMES)
    split = P(NAMES, None)
    return jax.shard_map(
        local, mesh=physical, in_specs=(split, split, split, P()), out_specs=split, check_vma=False
    )
```

```python
import math

import jax
import jax.numpy as jnp
from jax import lax
from jax.experimental import pallas as pl
from jax.experimental.pallas import tpu as pltpu
from jax.sharding import Mesh, PartitionSpec as P


ZL, X, ZH, Y, CORE = 6, 4, 2, 8, 2
NAMES = ("zl", "x", "zh", "y", "c")
Z_AXES = ("zl", "zh")
Z = ZL * ZH
UNLISTED = -1e30
LANES = 128
VMEM = pl.BlockSpec(memory_space=pltpu.VMEM)


def gather_direct(value, axes, count):
    copies = jnp.broadcast_to(value[None], (count,) + value.shape)
    gathered = lax.all_to_all(copies, axes, 0, 0, tiled=True)
    return gathered.reshape((count * value.shape[0],) + value.shape[1:])


def gather_by_permutes(value, axis, count):
    blocks = [value]
    for steps in range(1, count):
        pairs = [(source, (source + steps) % count) for source in range(count)]
        blocks.append(lax.ppermute(value, axis, pairs))
    return jnp.concatenate(blocks, axis=0)


def split3(value):
    high = value.astype(jnp.bfloat16)
    rest = value - high.astype(jnp.float32)
    middle = rest.astype(jnp.bfloat16)
    low = (rest - middle.astype(jnp.float32)).astype(jnp.bfloat16)
    return high, middle, low


def pack_stats(row_max, weight_sum, rows):
    lane = lax.broadcasted_iota(jnp.int32, (rows, LANES), 1)
    stats = jnp.zeros((rows, LANES), jnp.float32)
    for place, piece in enumerate(split3(row_max) + split3(weight_sum)):
        stats = jnp.where(lane == place, piece.astype(jnp.float32), stats)
    return stats.astype(jnp.bfloat16)


def score_kernel(queries_ref, own_ref, other_ref, bias_ref, out_ref, *, width, tile_rows, scale):
    rows = queries_ref.shape[0]
    lands = own_ref.shape[0]
    tiles = bias_ref.shape[1]
    chunk = tiles * tile_rows

    def step(index):
        start = pl.multiple_of(index * chunk, chunk)
        queries = queries_ref[pl.ds(start, chunk), :]
        bias = bias_ref[index]

        def logits_of(land_ref, first):
            logits = lax.dot_general(
                queries,
                land_ref[:, :width],
                (((1,), (1,)), ((), ())),
                preferred_element_type=jnp.float32,
            )
            logits = (logits * scale).reshape(tiles, tile_rows, lands)
            return (logits + bias[:, None, first : first + lands]).reshape(chunk, lands)

        own = logits_of(own_ref, 0)
        other = logits_of(other_ref, lands)
        row_max = jnp.max(jnp.maximum(own, other), axis=1, keepdims=True)
        own = jnp.exp(own - row_max)
        other = jnp.exp(other - row_max)
        weight_sum = jnp.sum(own + other, axis=1, keepdims=True)
        label_sum = jnp.dot(
            own.astype(jnp.bfloat16), own_ref[:, width:], preferred_element_type=jnp.float32
        ) + jnp.dot(
            other.astype(jnp.bfloat16), other_ref[:, width:], preferred_element_type=jnp.float32
        )
        out_ref[pl.ds(start, chunk), :LANES] = (label_sum / weight_sum).astype(jnp.bfloat16)
        out_ref[pl.ds(start, chunk), LANES:] = pack_stats(row_max, weight_sum, chunk)

    pl.loop(0, rows // chunk)(step)


def score(queries, own, other, bias, width, tile_rows, scale):
    rows = queries.shape[0]
    lands = own.shape[0] + other.shape[0]
    classes = own.shape[1] - width
    tiles = 8
    return pl.pallas_call(
        lambda *refs: score_kernel(*refs, width=width, tile_rows=tile_rows, scale=scale),
        out_shape=jax.ShapeDtypeStruct((rows, classes + LANES), jnp.bfloat16),
        in_specs=[VMEM] * 4,
        out_specs=VMEM,
        cost_estimate=pl.CostEstimate(
            flops=2 * rows * lands * (width + classes),
            bytes_accessed=2 * (rows * width + lands * (width + classes) + rows * 256),
            transcendentals=rows * lands,
        ),
        compiler_params=pltpu.CompilerParams(vmem_limit_bytes=24 << 20),
        name="score",
    )(queries, own, other, bias.reshape(rows // (tiles * tile_rows), tiles, lands))


def merge_kernel(parts_ref, out_ref):
    sources, rows, _ = parts_ref.shape
    piece = lax.broadcasted_iota(jnp.int32, (LANES, 2 * LANES), 0)
    lane = lax.broadcasted_iota(jnp.int32, (LANES, 2 * LANES), 1)
    first = jnp.where(lane < LANES, 0, 3)
    spread = jnp.where((piece >= first) & (piece < first + 3), 1.0, 0.0).astype(jnp.bfloat16)
    stats = [
        jnp.dot(parts_ref[source, :, LANES:], spread, preferred_element_type=jnp.float32)
        for source in range(sources)
    ]
    joint = stats[0][:, :LANES]
    for stat in stats[1:]:
        joint = jnp.maximum(joint, stat[:, :LANES])
    total = jnp.zeros((rows, LANES), jnp.float32)
    labels = jnp.zeros((rows, LANES), jnp.float32)
    for source, stat in enumerate(stats):
        weight = stat[:, LANES:] * jnp.exp(stat[:, :LANES] - joint)
        total = total + weight
        labels = labels + parts_ref[source, :, :LANES].astype(jnp.float32) * weight
    out_ref[:, :LANES] = (labels / total).astype(jnp.bfloat16)
    if out_ref.shape[1] > LANES:
        out_ref[:, LANES:] = pack_stats(joint, total, rows)


def merge(parts, width):
    return pl.pallas_call(
        merge_kernel,
        out_shape=jax.ShapeDtypeStruct((parts.shape[1], width), jnp.bfloat16),
        in_specs=[VMEM],
        out_specs=VMEM,
        compiler_params=pltpu.CompilerParams(vmem_limit_bytes=8 << 20),
        name="merge",
    )(parts)


def local(queries, landmarks, labels, tile_mask):
    rows, width = queries.shape
    tile_lands, classes = labels.shape
    scale = 4.0 / math.sqrt(width)
    gathered = gather_direct(queries, Z_AXES, Z)
    packed = jnp.concatenate([landmarks, labels], axis=1)
    own = gather_by_permutes(packed, "y", Y)
    other = lax.ppermute(own, "c", [(0, 1), (1, 0)])
    gathered = gather_direct(gathered, "x", X)

    place = lax.axis_index("zl") * X + lax.axis_index("x")
    first = (place * ZH + lax.axis_index("zh")) * (Y * CORE)
    steps = jnp.arange(Y, dtype=jnp.int32)
    behind = (lax.axis_index("y") - steps) % Y
    wanted = lax.axis_index("c") ^ jnp.arange(CORE, dtype=jnp.int32)
    tiles = (behind[None, :] * CORE + wanted[:, None]).reshape(1, CORE * Y)
    pick = tiles == lax.broadcasted_iota(jnp.int32, (Y * CORE, 1), 0)
    listed = lax.dynamic_slice_in_dim(tile_mask, first, Y * CORE, 1).astype(jnp.float32)
    listed = listed.reshape(ZL, X, Y * CORE).transpose(1, 0, 2).reshape(X * ZL, Y * CORE)
    pick = jnp.repeat(pick.astype(jnp.float32), tile_lands, axis=1)
    listed = jnp.dot(listed, pick, preferred_element_type=jnp.float32) > 0.5

    def half_norm(land):
        land_f = land[:, :width].astype(jnp.float32)
        return 0.5 * jnp.sum(land_f * land_f, axis=1)

    norms = jnp.concatenate([half_norm(own), half_norm(other)])
    bias = jnp.where(listed, -scale * norms[None, :], jnp.float32(UNLISTED))

    parts = score(gathered, own, other, bias, width, ZH * rows, scale)
    parts = lax.all_to_all(parts.reshape(X, Z * rows, classes + LANES), "x", 0, 0, tiled=True)
    parts = merge(parts, classes + LANES)
    parts = lax.all_to_all(parts.reshape(Z, rows, classes + LANES), Z_AXES, 0, 0, tiled=True)
    return merge(parts, classes)


def solution(mesh):
    physical = Mesh(mesh.devices.reshape(ZL, X, ZH, Y, CORE), NAMES)
    split = P(NAMES, None)

    return jax.shard_map(
        local, mesh=physical, in_specs=(split, split, split, P()), out_specs=split, check_vma=False
    )
```

```python
import math

import jax
import jax.numpy as jnp
from jax import lax
from jax.experimental import pallas as pl
from jax.experimental.pallas import tpu as pltpu
from jax.sharding import Mesh, PartitionSpec as P


ZL, X, ZH, Y, CORE = 6, 4, 2, 8, 2
NAMES = ("zl", "x", "zh", "y", "c")
Z_AXES = ("zl", "zh")
Z = ZL * ZH
UNLISTED = -1e30
LANES = 128
VMEM = pl.BlockSpec(memory_space=pltpu.VMEM)


def gather_direct(value, axes, count):
    copies = jnp.broadcast_to(value[None], (count,) + value.shape)
    gathered = lax.all_to_all(copies, axes, 0, 0, tiled=True)
    return gathered.reshape((count * value.shape[0],) + value.shape[1:])


def both_ways(value, steps):
    pairs = [
        (y * CORE + core, (y + (steps if core == 0 else -steps)) % Y * CORE + core)
        for y in range(Y)
        for core in range(CORE)
    ]
    return lax.ppermute(value, ("y", "c"), pairs)


def swap_cores(value):
    return lax.ppermute(value, "c", [(0, 1), (1, 0)])


def tiles_held():
    y, core = lax.axis_index("y"), lax.axis_index("c")
    steps = jnp.array([0, 1, 1, 2, 2, 3, 3, 4], jnp.int32)
    flip = jnp.array([0, 0, 1, 0, 1, 0, 1, 0], jnp.int32)

    def of(core):
        behind = jnp.where(core == 0, -steps, steps)
        return (y + behind) % Y * CORE + (core ^ flip)

    return jnp.concatenate([of(core), of(1 - core)])


def split3(value):
    high = value.astype(jnp.bfloat16)
    rest = value - high.astype(jnp.float32)
    middle = rest.astype(jnp.bfloat16)
    low = (rest - middle.astype(jnp.float32)).astype(jnp.bfloat16)
    return high, middle, low


def pack_stats(row_max, weight_sum, rows):
    lane = lax.broadcasted_iota(jnp.int32, (rows, LANES), 1)
    stats = jnp.zeros((rows, LANES), jnp.float32)
    for place, piece in enumerate(split3(row_max) + split3(weight_sum)):
        stats = jnp.where(lane == place, piece.astype(jnp.float32), stats)
    return stats.astype(jnp.bfloat16)


def score_kernel(queries_ref, own_ref, other_ref, bias_ref, out_ref, *, width, tile_rows, scale):
    rows = queries_ref.shape[0]
    lands = own_ref.shape[0]
    tiles = bias_ref.shape[1]
    chunk = tiles * tile_rows

    def step(index):
        start = pl.multiple_of(index * chunk, chunk)
        queries = queries_ref[pl.ds(start, chunk), :]
        bias = bias_ref[index]

        def logits_of(land_ref, first):
            logits = lax.dot_general(
                queries,
                land_ref[:, :width],
                (((1,), (1,)), ((), ())),
                preferred_element_type=jnp.float32,
            )
            logits = (logits * scale).reshape(tiles, tile_rows, lands)
            return (logits + bias[:, None, first : first + lands]).reshape(chunk, lands)

        own = logits_of(own_ref, 0)
        other = logits_of(other_ref, lands)
        row_max = jnp.max(jnp.maximum(own, other), axis=1, keepdims=True)
        own = jnp.exp(own - row_max)
        other = jnp.exp(other - row_max)
        weight_sum = jnp.sum(own + other, axis=1, keepdims=True)
        label_sum = jnp.dot(
            own.astype(jnp.bfloat16), own_ref[:, width:], preferred_element_type=jnp.float32
        ) + jnp.dot(
            other.astype(jnp.bfloat16), other_ref[:, width:], preferred_element_type=jnp.float32
        )
        out_ref[pl.ds(start, chunk), :LANES] = (label_sum / weight_sum).astype(jnp.bfloat16)
        out_ref[pl.ds(start, chunk), LANES:] = pack_stats(row_max, weight_sum, chunk)

    pl.loop(0, rows // chunk)(step)


def score(queries, own, other, bias, width, tile_rows, scale):
    rows = queries.shape[0]
    lands = own.shape[0] + other.shape[0]
    classes = own.shape[1] - width
    tiles = 8
    return pl.pallas_call(
        lambda *refs: score_kernel(*refs, width=width, tile_rows=tile_rows, scale=scale),
        out_shape=jax.ShapeDtypeStruct((rows, classes + LANES), jnp.bfloat16),
        in_specs=[VMEM] * 4,
        out_specs=VMEM,
        cost_estimate=pl.CostEstimate(
            flops=2 * rows * lands * (width + classes),
            bytes_accessed=2 * (rows * width + lands * (width + classes) + rows * 256),
            transcendentals=rows * lands,
        ),
        compiler_params=pltpu.CompilerParams(vmem_limit_bytes=24 << 20),
        name="score",
    )(queries, own, other, bias.reshape(rows // (tiles * tile_rows), tiles, lands))


def merge_kernel(parts_ref, out_ref):
    sources, rows, _ = parts_ref.shape
    piece = lax.broadcasted_iota(jnp.int32, (LANES, 2 * LANES), 0)
    lane = lax.broadcasted_iota(jnp.int32, (LANES, 2 * LANES), 1)
    first = jnp.where(lane < LANES, 0, 3)
    spread = jnp.where((piece >= first) & (piece < first + 3), 1.0, 0.0).astype(jnp.bfloat16)
    stats = [
        jnp.dot(parts_ref[source, :, LANES:], spread, preferred_element_type=jnp.float32)
        for source in range(sources)
    ]
    joint = stats[0][:, :LANES]
    for stat in stats[1:]:
        joint = jnp.maximum(joint, stat[:, :LANES])
    total = jnp.zeros((rows, LANES), jnp.float32)
    labels = jnp.zeros((rows, LANES), jnp.float32)
    for source, stat in enumerate(stats):
        weight = stat[:, LANES:] * jnp.exp(stat[:, :LANES] - joint)
        total = total + weight
        labels = labels + parts_ref[source, :, :LANES].astype(jnp.float32) * weight
    out_ref[:, :LANES] = (labels / total).astype(jnp.bfloat16)
    if out_ref.shape[1] > LANES:
        out_ref[:, LANES:] = pack_stats(joint, total, rows)


def merge(parts, width):
    return pl.pallas_call(
        merge_kernel,
        out_shape=jax.ShapeDtypeStruct((parts.shape[1], width), jnp.bfloat16),
        in_specs=[VMEM],
        out_specs=VMEM,
        compiler_params=pltpu.CompilerParams(vmem_limit_bytes=8 << 20),
        name="merge",
    )(parts)


def local(queries, landmarks, labels, tile_mask):
    rows, width = queries.shape
    tile_lands, classes = labels.shape
    scale = 4.0 / math.sqrt(width)
    mine = jnp.concatenate([landmarks, labels], axis=1)
    pair = jnp.concatenate([mine, swap_cores(mine)], axis=0)
    gathered = gather_direct(queries, Z_AXES, Z)
    third, fourth, second = both_ways(pair, 3), both_ways(mine, 4), both_ways(pair, 2)
    first = both_ways(pair, 1)
    own = jnp.concatenate([mine, first, second, third, fourth], axis=0)
    other = swap_cores(own)
    gathered = gather_direct(gathered, "x", X)

    place = lax.axis_index("zl") * X + lax.axis_index("x")
    start = (place * ZH + lax.axis_index("zh")) * (Y * CORE)
    pick = tiles_held()[None, :] == lax.broadcasted_iota(jnp.int32, (Y * CORE, 1), 0)
    listed = lax.dynamic_slice_in_dim(tile_mask, start, Y * CORE, 1).astype(jnp.float32)
    listed = listed.reshape(ZL, X, Y * CORE).transpose(1, 0, 2).reshape(X * ZL, Y * CORE)
    pick = jnp.repeat(pick.astype(jnp.float32), tile_lands, axis=1)
    listed = jnp.dot(listed, pick, preferred_element_type=jnp.float32) > 0.5

    def half_norm(land):
        land_f = land[:, :width].astype(jnp.float32)
        return 0.5 * jnp.sum(land_f * land_f, axis=1)

    norms = jnp.concatenate([half_norm(own), half_norm(other)])
    bias = jnp.where(listed, -scale * norms[None, :], jnp.float32(UNLISTED))

    parts = score(gathered, own, other, bias, width, ZH * rows, scale)
    parts = lax.all_to_all(parts.reshape(X, Z * rows, classes + LANES), "x", 0, 0, tiled=True)
    parts = merge(parts, classes + LANES)
    parts = lax.all_to_all(parts.reshape(Z, rows, classes + LANES), Z_AXES, 0, 0, tiled=True)
    return merge(parts, classes)


def solution(mesh):
    physical = Mesh(mesh.devices.reshape(ZL, X, ZH, Y, CORE), NAMES)
    split = P(NAMES, None)

    return jax.shard_map(
        local, mesh=physical, in_specs=(split, split, split, P()), out_specs=split, check_vma=False
    )
```

```python
import math

import jax
import jax.numpy as jnp
from jax import lax
from jax.experimental import pallas as pl
from jax.experimental.pallas import tpu as pltpu
from jax.sharding import Mesh, PartitionSpec as P


ZL, X, ZH, Y, CORE = 6, 4, 2, 8, 2
NAMES = ("zl", "x", "zh", "y", "c")
Z_AXES = ("zl", "zh")
Z = ZL * ZH
UNLISTED = -1e30
LANES = 128
VMEM = pl.BlockSpec(memory_space=pltpu.VMEM)


def gather_direct(value, axes, count):
    copies = jnp.broadcast_to(value[None], (count,) + value.shape)
    gathered = lax.all_to_all(copies, axes, 0, 0, tiled=True)
    return gathered.reshape((count * value.shape[0],) + value.shape[1:])


def both_ways(value, steps):
    pairs = [
        (y * CORE + core, (y + (steps if core == 0 else -steps)) % Y * CORE + core)
        for y in range(Y)
        for core in range(CORE)
    ]
    return lax.ppermute(value, ("y", "c"), pairs)


def swap_cores(value):
    return lax.ppermute(value, "c", [(0, 1), (1, 0)])


def tiles_held():
    y, core = lax.axis_index("y"), lax.axis_index("c")
    steps = jnp.array([0, 1, 1, 2, 2, 3, 3, 4], jnp.int32)
    flip = jnp.array([0, 0, 1, 0, 1, 0, 1, 0], jnp.int32)

    def of(core):
        behind = jnp.where(core == 0, -steps, steps)
        return (y + behind) % Y * CORE + (core ^ flip)

    return jnp.concatenate([of(core), of(1 - core)])


def split3(value):
    high = value.astype(jnp.bfloat16)
    rest = value - high.astype(jnp.float32)
    middle = rest.astype(jnp.bfloat16)
    low = (rest - middle.astype(jnp.float32)).astype(jnp.bfloat16)
    return high, middle, low


def stats_rows(row_max, weight_sum, dests, rows):
    lane = lax.broadcasted_iota(jnp.int32, (dests * rows, LANES), 1)
    row = lax.broadcasted_iota(jnp.int32, (dests * rows, LANES), 0) % rows
    stats = jnp.zeros((dests * rows, LANES), jnp.float32)
    for place, piece in enumerate(split3(row_max) + split3(weight_sum)):
        stats = jnp.where(lane // rows == place, piece.astype(jnp.float32), stats)
    stats = jnp.where(lane % rows == row, stats, 0.0)
    return jnp.sum(stats.reshape(dests, rows, LANES), axis=1, keepdims=True)


def score_kernel(queries_ref, own_ref, other_ref, bias_ref, out_ref, *, width, tile_rows, part_rows, scale):
    rows = queries_ref.shape[0]
    lands = own_ref.shape[0]
    tiles = bias_ref.shape[1]
    chunk = tiles * tile_rows

    def step(index):
        start = pl.multiple_of(index * chunk, chunk)
        queries = queries_ref[pl.ds(start, chunk), :]
        bias = bias_ref[index]

        def logits_of(land_ref, first):
            logits = lax.dot_general(
                queries,
                land_ref[:, :width],
                (((1,), (1,)), ((), ())),
                preferred_element_type=jnp.float32,
            )
            logits = (logits * scale).reshape(tiles, tile_rows, lands)
            return (logits + bias[:, None, first : first + lands]).reshape(chunk, lands)

        own = logits_of(own_ref, 0)
        other = logits_of(other_ref, lands)
        row_max = jnp.max(jnp.maximum(own, other), axis=1, keepdims=True)
        own = jnp.exp(own - row_max)
        other = jnp.exp(other - row_max)
        weight_sum = jnp.sum(own + other, axis=1, keepdims=True)
        label_sum = jnp.dot(
            own.astype(jnp.bfloat16), own_ref[:, width:], preferred_element_type=jnp.float32
        ) + jnp.dot(
            other.astype(jnp.bfloat16), other_ref[:, width:], preferred_element_type=jnp.float32
        )
        dests = chunk // part_rows
        place = pl.ds(pl.multiple_of(index * dests, dests), dests)
        scores = (label_sum / weight_sum).astype(jnp.bfloat16)
        out_ref[place, :part_rows, :] = scores.reshape(dests, part_rows, LANES)
        stats = stats_rows(row_max, weight_sum, dests, part_rows)
        out_ref[place, part_rows:, :] = jnp.broadcast_to(stats, (dests, 8, LANES)).astype(jnp.bfloat16)

    pl.loop(0, rows // chunk)(step)


def score(queries, own, other, bias, width, tile_rows, part_rows, scale):
    rows = queries.shape[0]
    lands = own.shape[0] + other.shape[0]
    classes = own.shape[1] - width
    tiles = 8
    return pl.pallas_call(
        lambda *refs: score_kernel(
            *refs, width=width, tile_rows=tile_rows, part_rows=part_rows, scale=scale
        ),
        out_shape=jax.ShapeDtypeStruct((rows // part_rows, part_rows + 8, classes), jnp.bfloat16),
        in_specs=[VMEM] * 4,
        out_specs=VMEM,
        cost_estimate=pl.CostEstimate(
            flops=2 * rows * lands * (width + classes),
            bytes_accessed=2 * (rows * width + lands * (width + classes) + rows * 192),
            transcendentals=rows * lands,
        ),
        compiler_params=pltpu.CompilerParams(vmem_limit_bytes=24 << 20),
        name="score",
    )(queries, own, other, bias.reshape(rows // (tiles * tile_rows), tiles, lands))


def merge_kernel(parts_ref, out_ref):
    sources = parts_ref.shape[0]
    rows = out_ref.shape[0]
    lane = lax.broadcasted_iota(jnp.int32, (1, rows, LANES), 2)
    row = lax.broadcasted_iota(jnp.int32, (1, rows, LANES), 1)
    stats = parts_ref[:, rows:, :].astype(jnp.float32)
    stats = jnp.concatenate([stats] * (rows // 8), axis=1)
    stats = jnp.where(lane % rows == row, stats, 0.0).astype(jnp.bfloat16)
    piece = lax.broadcasted_iota(jnp.int32, (LANES, 2 * LANES), 0) // rows
    half = lax.broadcasted_iota(jnp.int32, (LANES, 2 * LANES), 1) // LANES
    spread = jnp.where(piece // 3 == half, 1.0, 0.0).astype(jnp.bfloat16)
    stats = jnp.dot(
        stats.reshape(sources * rows, LANES), spread, preferred_element_type=jnp.float32
    ).reshape(sources, rows, 2 * LANES)
    row_max = stats[:, :, :LANES]
    weight = stats[:, :, LANES:] * jnp.exp(row_max - jnp.max(row_max, axis=0, keepdims=True))
    labels = jnp.sum(parts_ref[:, :rows, :].astype(jnp.float32) * weight, axis=0)
    out_ref[...] = (labels / jnp.sum(weight, axis=0)).astype(jnp.bfloat16)


def merge(parts, rows):
    return pl.pallas_call(
        merge_kernel,
        out_shape=jax.ShapeDtypeStruct((rows, parts.shape[2]), jnp.bfloat16),
        in_specs=[VMEM],
        out_specs=VMEM,
        compiler_params=pltpu.CompilerParams(vmem_limit_bytes=8 << 20),
        name="merge",
    )(parts)


def local(queries, landmarks, labels, tile_mask):
    rows, width = queries.shape
    tile_lands, _ = labels.shape
    scale = 4.0 / math.sqrt(width)
    mine = jnp.concatenate([landmarks, labels], axis=1)
    pair = jnp.concatenate([mine, swap_cores(mine)], axis=0)
    gathered = gather_direct(queries, Z_AXES, Z)
    second, first = both_ways(pair, 2), both_ways(pair, 1)
    relayed = both_ways(jnp.concatenate([first, second[:tile_lands]], axis=0), 2)
    own = jnp.concatenate([mine, first, second, relayed], axis=0)
    other = swap_cores(own)
    gathered = gather_direct(gathered, "x", X)

    place = lax.axis_index("zl") * X + lax.axis_index("x")
    start = (place * ZH + lax.axis_index("zh")) * (Y * CORE)
    pick = tiles_held()[None, :] == lax.broadcasted_iota(jnp.int32, (Y * CORE, 1), 0)
    listed = lax.dynamic_slice_in_dim(tile_mask, start, Y * CORE, 1).astype(jnp.float32)
    listed = listed.reshape(ZL, X, Y * CORE).transpose(1, 0, 2).reshape(X * ZL, Y * CORE)
    pick = jnp.repeat(pick.astype(jnp.float32), tile_lands, axis=1)
    listed = jnp.dot(listed, pick, preferred_element_type=jnp.float32) > 0.5

    def half_norm(land):
        land_f = land[:, :width].astype(jnp.float32)
        return 0.5 * jnp.sum(land_f * land_f, axis=1)

    norms = jnp.concatenate([half_norm(own), half_norm(other)])
    bias = jnp.where(listed, -scale * norms[None, :], jnp.float32(UNLISTED))

    parts = score(gathered, own, other, bias, width, ZH * rows, rows, scale)
    parts = lax.all_to_all(parts, ("x",) + Z_AXES, 0, 0, tiled=True)
    return merge(parts, rows)


def solution(mesh):
    physical = Mesh(mesh.devices.reshape(ZL, X, ZH, Y, CORE), NAMES)
    split = P(NAMES, None)

    return jax.shard_map(
        local, mesh=physical, in_specs=(split, split, split, P()), out_specs=split, check_vma=False
    )
```

```python
import math

import jax
import jax.numpy as jnp
from jax import lax
from jax.experimental import pallas as pl
from jax.experimental.pallas import tpu as pltpu
from jax.sharding import Mesh, PartitionSpec as P


ZL, X, ZH, Y, CORE = 6, 4, 2, 8, 2
NAMES = ("zl", "x", "zh", "y", "c")
Z = ZL * ZH
UNLISTED = -1e30
LANES = 128
VMEM = pl.BlockSpec(memory_space=pltpu.VMEM)


def gather_direct(value, axes, count):
    copies = jnp.broadcast_to(value[None], (count,) + value.shape)
    gathered = lax.all_to_all(copies, axes, 0, 0, tiled=True)
    return gathered.reshape((count * value.shape[0],) + value.shape[1:])


def pass_on(tile):
    pairs = []
    for z in range(Z):
        for core in range(CORE):
            to = (z + (1 if core == 0 else -1)) % Z
            pairs.append(tuple((at % ZL * ZH + at // ZL) * CORE + core for at in (z, to)))
    return lax.ppermute(tile, ("zl", "zh", "c"), pairs)


def swap_cores(value):
    return lax.ppermute(value, "c", [(0, 1), (1, 0)])


def tiles_held():
    core = lax.axis_index("c")
    place = lax.broadcasted_iota(jnp.int32, (Z,), 0)
    steps = (place + 1) // 2
    flip = jnp.where(place == 0, 0, 1 - place % 2)
    z = lax.axis_index("zh") * ZL + lax.axis_index("zl")
    z = (z + jnp.where(core == 0, Z - steps, steps)) % Z
    loop = z % ZL * X + lax.axis_index("x")
    return ((loop * ZH + z // ZL) * Y + lax.axis_index("y")) * CORE + (core ^ flip)


def split3(value):
    high = value.astype(jnp.bfloat16)
    rest = value - high.astype(jnp.float32)
    middle = rest.astype(jnp.bfloat16)
    low = (rest - middle.astype(jnp.float32)).astype(jnp.bfloat16)
    return high, middle, low


def stats_rows(row_max, weight_sum, dests, rows):
    lane = lax.broadcasted_iota(jnp.int32, (dests * rows, LANES), 1)
    row = lax.broadcasted_iota(jnp.int32, (dests * rows, LANES), 0) % rows
    stats = jnp.zeros((dests * rows, LANES), jnp.float32)
    for place, piece in enumerate(split3(row_max) + split3(weight_sum)):
        stats = jnp.where(lane // rows == place, piece.astype(jnp.float32), stats)
    stats = jnp.where(lane % rows == row, stats, 0.0)
    return jnp.sum(stats.reshape(dests, rows, LANES), axis=1, keepdims=True)


def score_kernel(
    queries_ref, own_ref, other_ref, own_bias_ref, other_bias_ref, out_ref, *, width, part_rows, scale
):
    tiles = own_bias_ref.shape[0]
    chunk = queries_ref.shape[0] // tiles
    dests = chunk // part_rows

    for tile in range(tiles):
        queries = queries_ref[tile * chunk : (tile + 1) * chunk, :]

        def logits_of(land_ref, bias_ref):
            logits = lax.dot_general(
                queries,
                land_ref[:, :width],
                (((1,), (1,)), ((), ())),
                preferred_element_type=jnp.float32,
            )
            return logits * scale + bias_ref[tile : tile + 1, :]

        own = logits_of(own_ref, own_bias_ref)
        other = logits_of(other_ref, other_bias_ref)
        row_max = jnp.max(jnp.maximum(own, other), axis=1, keepdims=True)
        own = jnp.exp(own - row_max)
        other = jnp.exp(other - row_max)
        weight_sum = jnp.sum(own + other, axis=1, keepdims=True)
        label_sum = jnp.dot(
            own.astype(jnp.bfloat16), own_ref[:, width:], preferred_element_type=jnp.float32
        ) + jnp.dot(
            other.astype(jnp.bfloat16), other_ref[:, width:], preferred_element_type=jnp.float32
        )
        place = slice(tile * dests, (tile + 1) * dests)
        scores = (label_sum / weight_sum).astype(jnp.bfloat16)
        out_ref[place, :part_rows, :] = scores.reshape(dests, part_rows, LANES)
        stats = stats_rows(row_max, weight_sum, dests, part_rows)
        out_ref[place, part_rows:, :] = jnp.broadcast_to(stats, (dests, 8, LANES)).astype(jnp.bfloat16)


def score(queries, own, other, own_bias, other_bias, width, part_rows, scale):
    rows = queries.shape[0]
    lands = own.shape[0] + other.shape[0]
    classes = own.shape[1] - width
    return pl.pallas_call(
        lambda *refs: score_kernel(*refs, width=width, part_rows=part_rows, scale=scale),
        out_shape=jax.ShapeDtypeStruct((rows // part_rows, part_rows + 8, classes), jnp.bfloat16),
        in_specs=[VMEM] * 5,
        out_specs=VMEM,
        cost_estimate=pl.CostEstimate(
            flops=2 * rows * lands * (width + classes),
            bytes_accessed=2 * (rows * width + lands * (width + classes) + rows * 192),
            transcendentals=rows * lands,
        ),
        compiler_params=pltpu.CompilerParams(vmem_limit_bytes=24 << 20),
        name="score",
    )(queries, own, other, own_bias, other_bias)


def merge_kernel(parts_ref, out_ref):
    sources = parts_ref.shape[0]
    rows = out_ref.shape[0]
    lane = lax.broadcasted_iota(jnp.int32, (1, rows, LANES), 2)
    row = lax.broadcasted_iota(jnp.int32, (1, rows, LANES), 1)
    stats = parts_ref[:, rows:, :].astype(jnp.float32)
    stats = jnp.concatenate([stats] * (rows // 8), axis=1)
    stats = jnp.where(lane % rows == row, stats, 0.0).astype(jnp.bfloat16)
    piece = lax.broadcasted_iota(jnp.int32, (LANES, 2 * LANES), 0) // rows
    half = lax.broadcasted_iota(jnp.int32, (LANES, 2 * LANES), 1) // LANES
    spread = jnp.where(piece // 3 == half, 1.0, 0.0).astype(jnp.bfloat16)
    stats = jnp.dot(
        stats.reshape(sources * rows, LANES), spread, preferred_element_type=jnp.float32
    ).reshape(sources, rows, 2 * LANES)
    row_max = stats[:, :, :LANES]
    weight = stats[:, :, LANES:] * jnp.exp(row_max - jnp.max(row_max, axis=0, keepdims=True))
    labels = jnp.sum(parts_ref[:, :rows, :].astype(jnp.float32) * weight, axis=0)
    out_ref[...] = (labels / jnp.sum(weight, axis=0)).astype(jnp.bfloat16)


def merge(parts, rows):
    return pl.pallas_call(
        merge_kernel,
        out_shape=jax.ShapeDtypeStruct((rows, parts.shape[2]), jnp.bfloat16),
        in_specs=[VMEM],
        out_specs=VMEM,
        compiler_params=pltpu.CompilerParams(vmem_limit_bytes=8 << 20),
        name="merge",
    )(parts)


def local(queries, landmarks, labels, tile_mask):
    rows, width = queries.shape
    tile_lands, classes = labels.shape
    scale = 4.0 / math.sqrt(width)
    mine = jnp.concatenate([landmarks, labels], axis=1)
    gathered = gather_direct(queries, ("x", "y"), X * Y)

    own = jnp.zeros((Z * tile_lands, width + classes), jnp.bfloat16)
    own = lax.dynamic_update_slice_in_dim(own, mine, 0, 0)
    chains = [mine, swap_cores(mine)]
    for place in range(1, Z):
        chain = (place + 1) % 2
        chains[chain] = pass_on(chains[chain])
        own = lax.dynamic_update_slice_in_dim(own, chains[chain], place * tile_lands, 0)
    other = swap_cores(own)

    wanted = lax.dynamic_slice_in_dim(tile_mask, lax.axis_index("zl") * X, X, 0)
    pick = lax.broadcasted_iota(jnp.int32, (tile_mask.shape[1], 1), 0) == tiles_held()[None, :]
    listed = jnp.dot(
        wanted.astype(jnp.float32), pick.astype(jnp.float32), preferred_element_type=jnp.float32
    )
    listed = jnp.broadcast_to(listed[:, :, None] > 0.5, (X, Z, tile_lands)).reshape(X, Z * tile_lands)
    own_f = own[:, :width].astype(jnp.float32)
    half_norm = 0.5 * jnp.sum(own_f * own_f, axis=1)
    own_bias = jnp.where(listed, -scale * half_norm[None, :], jnp.float32(UNLISTED))
    other_bias = swap_cores(own_bias)

    parts = score(gathered, own, other, own_bias, other_bias, width, rows, scale)
    parts = lax.all_to_all(parts, ("x", "y"), 0, 0, tiled=True)
    return merge(parts, rows)


def solution(mesh):
    physical = Mesh(mesh.devices.reshape(ZL, X, ZH, Y, CORE), NAMES)
    split = P(NAMES, None)

    return jax.shard_map(
        local, mesh=physical, in_specs=(split, split, split, P()), out_specs=split, check_vma=False
    )
```

```python
import math

import jax
import jax.numpy as jnp
from jax import lax
from jax.experimental import pallas as pl
from jax.experimental.pallas import tpu as pltpu
from jax.sharding import Mesh, PartitionSpec as P


ZL, X, ZH, Y, CORE = 6, 4, 2, 8, 2
NAMES = ("zl", "x", "zh", "y", "c")
Z_AXES = ("zl", "zh")
Z = ZL * ZH
UNLISTED = -1e30
LANES = 128
VMEM = pl.BlockSpec(memory_space=pltpu.VMEM)


def gather_direct(value, axes, count):
    copies = jnp.broadcast_to(value[None], (count,) + value.shape)
    gathered = lax.all_to_all(copies, axes, 0, 0, tiled=True)
    return gathered.reshape((count * value.shape[0],) + value.shape[1:])


def pass_on(tiles):
    pairs = []
    for y in range(Y):
        for core in range(CORE):
            to = (y + (1 if core == 0 else -1)) % Y
            pairs.append((y * CORE + core, to * CORE + core))
    return lax.ppermute(tiles, ("y", "c"), pairs)


def swap_cores(value):
    return lax.ppermute(value, "c", [(0, 1), (1, 0)])


def tiles_held():
    core = lax.axis_index("c")
    place = lax.broadcasted_iota(jnp.int32, (Y,), 0)
    steps = (place + 1) // 2
    flip = jnp.where(place == 0, 0, 1 - place % 2)
    y = (lax.axis_index("y") + jnp.where(core == 0, Y - steps, steps)) % Y
    return y * CORE + (core ^ flip)


def split3(value):
    high = value.astype(jnp.bfloat16)
    rest = value - high.astype(jnp.float32)
    middle = rest.astype(jnp.bfloat16)
    low = (rest - middle.astype(jnp.float32)).astype(jnp.bfloat16)
    return high, middle, low


def stats_rows(row_max, weight_sum, dests, rows):
    lane = lax.broadcasted_iota(jnp.int32, (dests * rows, LANES), 1)
    row = lax.broadcasted_iota(jnp.int32, (dests * rows, LANES), 0) % rows
    stats = jnp.zeros((dests * rows, LANES), jnp.float32)
    for place, piece in enumerate(split3(row_max) + split3(weight_sum)):
        stats = jnp.where(lane // rows == place, piece.astype(jnp.float32), stats)
    stats = jnp.where(lane % rows == row, stats, 0.0)
    return jnp.sum(stats.reshape(dests, rows, LANES), axis=1, keepdims=True)


def score_kernel(
    queries_ref, own_ref, other_ref, own_bias_ref, other_bias_ref, out_ref, *, width, tile_rows, part_rows, scale
):
    rows = queries_ref.shape[0]
    lands = own_ref.shape[0]
    tiles = own_bias_ref.shape[1]
    chunk = tiles * tile_rows

    def step(index):
        start = pl.multiple_of(index * chunk, chunk)
        queries = queries_ref[pl.ds(start, chunk), :]

        def logits_of(land_ref, bias_ref):
            logits = lax.dot_general(
                queries,
                land_ref[:, :width],
                (((1,), (1,)), ((), ())),
                preferred_element_type=jnp.float32,
            )
            logits = (logits * scale).reshape(tiles, tile_rows, lands)
            return (logits + bias_ref[index][:, None, :]).reshape(chunk, lands)

        own = logits_of(own_ref, own_bias_ref)
        other = logits_of(other_ref, other_bias_ref)
        row_max = jnp.max(jnp.maximum(own, other), axis=1, keepdims=True)
        own = jnp.exp(own - row_max)
        other = jnp.exp(other - row_max)
        weight_sum = jnp.sum(own + other, axis=1, keepdims=True)
        label_sum = jnp.dot(
            own.astype(jnp.bfloat16), own_ref[:, width:], preferred_element_type=jnp.float32
        ) + jnp.dot(
            other.astype(jnp.bfloat16), other_ref[:, width:], preferred_element_type=jnp.float32
        )
        dests = chunk // part_rows
        place = pl.ds(pl.multiple_of(index * dests, dests), dests)
        scores = (label_sum / weight_sum).astype(jnp.bfloat16)
        out_ref[place, :part_rows, :] = scores.reshape(dests, part_rows, LANES)
        stats = stats_rows(row_max, weight_sum, dests, part_rows)
        out_ref[place, part_rows:, :] = jnp.broadcast_to(stats, (dests, 8, LANES)).astype(jnp.bfloat16)

    pl.loop(0, rows // chunk)(step)


def score(queries, own, other, own_bias, other_bias, width, tile_rows, part_rows, scale):
    rows = queries.shape[0]
    lands = own.shape[0] + other.shape[0]
    classes = own.shape[1] - width
    return pl.pallas_call(
        lambda *refs: score_kernel(
            *refs, width=width, tile_rows=tile_rows, part_rows=part_rows, scale=scale
        ),
        out_shape=jax.ShapeDtypeStruct((rows // part_rows, part_rows + 8, classes), jnp.bfloat16),
        in_specs=[VMEM] * 5,
        out_specs=VMEM,
        cost_estimate=pl.CostEstimate(
            flops=2 * rows * lands * (width + classes),
            bytes_accessed=2 * (rows * width + lands * (width + classes) + rows * 192),
            transcendentals=rows * lands,
        ),
        compiler_params=pltpu.CompilerParams(vmem_limit_bytes=24 << 20),
        name="score",
    )(queries, own, other, own_bias, other_bias)


def merge_kernel(parts_ref, out_ref):
    sources = parts_ref.shape[0]
    rows = out_ref.shape[0]
    lane = lax.broadcasted_iota(jnp.int32, (1, rows, LANES), 2)
    row = lax.broadcasted_iota(jnp.int32, (1, rows, LANES), 1)
    stats = parts_ref[:, rows:, :].astype(jnp.float32)
    stats = jnp.concatenate([stats] * (rows // 8), axis=1)
    stats = jnp.where(lane % rows == row, stats, 0.0).astype(jnp.bfloat16)
    piece = lax.broadcasted_iota(jnp.int32, (LANES, 2 * LANES), 0) // rows
    half = lax.broadcasted_iota(jnp.int32, (LANES, 2 * LANES), 1) // LANES
    spread = jnp.where(piece // 3 == half, 1.0, 0.0).astype(jnp.bfloat16)
    stats = jnp.dot(
        stats.reshape(sources * rows, LANES), spread, preferred_element_type=jnp.float32
    ).reshape(sources, rows, 2 * LANES)
    row_max = stats[:, :, :LANES]
    weight = stats[:, :, LANES:] * jnp.exp(row_max - jnp.max(row_max, axis=0, keepdims=True))
    labels = jnp.sum(parts_ref[:, :rows, :].astype(jnp.float32) * weight, axis=0)
    out_ref[...] = (labels / jnp.sum(weight, axis=0)).astype(jnp.bfloat16)


def merge(parts, rows):
    return pl.pallas_call(
        merge_kernel,
        out_shape=jax.ShapeDtypeStruct((rows, parts.shape[2]), jnp.bfloat16),
        in_specs=[VMEM],
        out_specs=VMEM,
        compiler_params=pltpu.CompilerParams(vmem_limit_bytes=8 << 20),
        name="merge",
    )(parts)


def local(queries, landmarks, labels, tile_mask):
    rows, width = queries.shape
    tile_lands, classes = labels.shape
    scale = 4.0 / math.sqrt(width)
    mine = jnp.concatenate([landmarks, labels], axis=1)
    gathered = gather_direct(queries, Z_AXES, Z)
    place = lax.axis_index("zl") * X + lax.axis_index("x")
    start = (place * ZH + lax.axis_index("zh")) * (Y * CORE)
    pick = tiles_held()[None, :] == lax.broadcasted_iota(jnp.int32, (Y * CORE, 1), 0)
    listed = lax.dynamic_slice_in_dim(tile_mask, start, Y * CORE, 1).astype(jnp.float32)
    listed = listed.reshape(ZL, X, Y * CORE).transpose(1, 0, 2).reshape(X * ZL, Y * CORE)
    pick = jnp.repeat(pick.astype(jnp.float32), tile_lands, axis=1)
    listed = jnp.dot(listed, pick, preferred_element_type=jnp.float32)

    passing = jnp.concatenate([mine, swap_cores(mine)], axis=0)
    own = jnp.zeros((Y * tile_lands, width + classes), jnp.bfloat16)
    own = lax.dynamic_update_slice_in_dim(own, mine, 0, 0)
    for hop in range(1, Y // 2 + 1):
        if hop == 2:
            passing, listed = lax.optimization_barrier((passing, listed))
        if hop == Y // 2:
            passing = passing[:tile_lands]
        passing = pass_on(passing)
        own = lax.dynamic_update_slice_in_dim(own, passing, (2 * hop - 1) * tile_lands, 0)
    other = swap_cores(own)
    gathered = gather_direct(gathered, "x", X)

    own_f = own[:, :width].astype(jnp.float32)
    half_norm = 0.5 * jnp.sum(own_f * own_f, axis=1)
    listed = listed.reshape(X * ZL // 8, 8, Y * tile_lands) > 0.5
    own_bias = jnp.where(listed, -scale * half_norm[None, None, :], jnp.float32(UNLISTED))
    other_bias = swap_cores(own_bias)

    parts = score(gathered, own, other, own_bias, other_bias, width, ZH * rows, rows, scale)
    parts = lax.all_to_all(parts, ("x",) + Z_AXES, 0, 0, tiled=True)
    return merge(parts, rows)


def solution(mesh):
    physical = Mesh(mesh.devices.reshape(ZL, X, ZH, Y, CORE), NAMES)
    split = P(NAMES, None)

    return jax.shard_map(
        local, mesh=physical, in_specs=(split, split, split, P()), out_specs=split, check_vma=False
    )
```

```python
import math

import jax
import jax.numpy as jnp
from jax import lax
from jax.experimental import pallas as pl
from jax.experimental.pallas import tpu as pltpu
from jax.sharding import Mesh, PartitionSpec as P


ZL, X, ZH, Y, CORE = 6, 4, 2, 8, 2
NAMES = ("zl", "x", "zh", "y", "c")
Z_AXES = ("zl", "zh")
Z = ZL * ZH
UNLISTED = -1e30
LANES = 128
VMEM = pl.BlockSpec(memory_space=pltpu.VMEM)


def gather_direct(value, axes, count):
    copies = jnp.broadcast_to(value[None], (count,) + value.shape)
    gathered = lax.all_to_all(copies, axes, 0, 0, tiled=True)
    return gathered.reshape((count * value.shape[0],) + value.shape[1:])


def send_on(tiles, chips):
    pairs = []
    for y in range(Y):
        for core in range(CORE):
            to = (y + (chips if core == 0 else -chips)) % Y
            pairs.append((y * CORE + core, to * CORE + core))
    return lax.ppermute(tiles, ("y", "c"), pairs)


def swap_cores(value):
    return lax.ppermute(value, "c", [(0, 1), (1, 0)])


def tiles_held():
    core = lax.axis_index("c")
    place = lax.broadcasted_iota(jnp.int32, (Y,), 0)
    steps = (place + 1) // 2
    flip = jnp.where(place == 0, 0, 1 - place % 2)
    y = (lax.axis_index("y") + jnp.where(core == 0, Y - steps, steps)) % Y
    return y * CORE + (core ^ flip)


def split3(value):
    high = value.astype(jnp.bfloat16)
    rest = value - high.astype(jnp.float32)
    middle = rest.astype(jnp.bfloat16)
    low = (rest - middle.astype(jnp.float32)).astype(jnp.bfloat16)
    return high, middle, low


def stats_rows(row_max, weight_sum, dests, rows):
    lane = lax.broadcasted_iota(jnp.int32, (dests * rows, LANES), 1)
    row = lax.broadcasted_iota(jnp.int32, (dests * rows, LANES), 0) % rows
    stats = jnp.zeros((dests * rows, LANES), jnp.float32)
    for place, piece in enumerate(split3(row_max) + split3(weight_sum)):
        stats = jnp.where(lane // rows == place, piece.astype(jnp.float32), stats)
    stats = jnp.where(lane % rows == row, stats, 0.0)
    return jnp.sum(stats.reshape(dests, rows, LANES), axis=1, keepdims=True)


def score_kernel(
    queries_ref, own_ref, other_ref, own_bias_ref, other_bias_ref, out_ref, *, width, tile_rows, part_rows, scale
):
    rows = queries_ref.shape[0]
    lands = own_ref.shape[0]
    tiles = own_bias_ref.shape[1]
    chunk = tiles * tile_rows

    def step(index):
        start = pl.multiple_of(index * chunk, chunk)
        queries = queries_ref[pl.ds(start, chunk), :]

        def logits_of(land_ref, bias_ref):
            logits = lax.dot_general(
                queries,
                land_ref[:, :width],
                (((1,), (1,)), ((), ())),
                preferred_element_type=jnp.float32,
            )
            logits = (logits * scale).reshape(tiles, tile_rows, lands)
            return (logits + bias_ref[index][:, None, :]).reshape(chunk, lands)

        own = logits_of(own_ref, own_bias_ref)
        other = logits_of(other_ref, other_bias_ref)
        row_max = jnp.max(jnp.maximum(own, other), axis=1, keepdims=True)
        own = jnp.exp(own - row_max)
        other = jnp.exp(other - row_max)
        weight_sum = jnp.sum(own + other, axis=1, keepdims=True)
        label_sum = jnp.dot(
            own.astype(jnp.bfloat16), own_ref[:, width:], preferred_element_type=jnp.float32
        ) + jnp.dot(
            other.astype(jnp.bfloat16), other_ref[:, width:], preferred_element_type=jnp.float32
        )
        dests = chunk // part_rows
        place = pl.ds(pl.multiple_of(index * dests, dests), dests)
        scores = (label_sum / weight_sum).astype(jnp.bfloat16)
        out_ref[place, :part_rows, :] = scores.reshape(dests, part_rows, LANES)
        stats = stats_rows(row_max, weight_sum, dests, part_rows)
        out_ref[place, part_rows:, :] = jnp.broadcast_to(stats, (dests, 8, LANES)).astype(jnp.bfloat16)

    pl.loop(0, rows // chunk)(step)


def score(queries, own, other, own_bias, other_bias, width, tile_rows, part_rows, scale):
    rows = queries.shape[0]
    lands = own.shape[0] + other.shape[0]
    classes = own.shape[1] - width
    return pl.pallas_call(
        lambda *refs: score_kernel(
            *refs, width=width, tile_rows=tile_rows, part_rows=part_rows, scale=scale
        ),
        out_shape=jax.ShapeDtypeStruct((rows // part_rows, part_rows + 8, classes), jnp.bfloat16),
        in_specs=[VMEM] * 5,
        out_specs=VMEM,
        cost_estimate=pl.CostEstimate(
            flops=2 * rows * lands * (width + classes),
            bytes_accessed=2 * (rows * width + lands * (width + classes) + rows * 192),
            transcendentals=rows * lands,
        ),
        compiler_params=pltpu.CompilerParams(vmem_limit_bytes=24 << 20),
        name="score",
    )(queries, own, other, own_bias, other_bias)


def merge_kernel(parts_ref, out_ref):
    sources = parts_ref.shape[0]
    rows = out_ref.shape[0]
    lane = lax.broadcasted_iota(jnp.int32, (1, rows, LANES), 2)
    row = lax.broadcasted_iota(jnp.int32, (1, rows, LANES), 1)
    stats = parts_ref[:, rows:, :].astype(jnp.float32)
    stats = jnp.concatenate([stats] * (rows // 8), axis=1)
    stats = jnp.where(lane % rows == row, stats, 0.0).astype(jnp.bfloat16)
    piece = lax.broadcasted_iota(jnp.int32, (LANES, 2 * LANES), 0) // rows
    half = lax.broadcasted_iota(jnp.int32, (LANES, 2 * LANES), 1) // LANES
    spread = jnp.where(piece // 3 == half, 1.0, 0.0).astype(jnp.bfloat16)
    stats = jnp.dot(
        stats.reshape(sources * rows, LANES), spread, preferred_element_type=jnp.float32
    ).reshape(sources, rows, 2 * LANES)
    row_max = stats[:, :, :LANES]
    weight = stats[:, :, LANES:] * jnp.exp(row_max - jnp.max(row_max, axis=0, keepdims=True))
    labels = jnp.sum(parts_ref[:, :rows, :].astype(jnp.float32) * weight, axis=0)
    out_ref[...] = (labels / jnp.sum(weight, axis=0)).astype(jnp.bfloat16)


def merge(parts, rows):
    return pl.pallas_call(
        merge_kernel,
        out_shape=jax.ShapeDtypeStruct((rows, parts.shape[2]), jnp.bfloat16),
        in_specs=[VMEM],
        out_specs=VMEM,
        compiler_params=pltpu.CompilerParams(vmem_limit_bytes=8 << 20),
        name="merge",
    )(parts)


def local(queries, landmarks, labels, tile_mask):
    rows, width = queries.shape
    tile_lands, classes = labels.shape
    scale = 4.0 / math.sqrt(width)
    mine = jnp.concatenate([landmarks, labels], axis=1)
    gathered = gather_direct(queries, Z_AXES, Z)
    place = lax.axis_index("zl") * X + lax.axis_index("x")
    start = (place * ZH + lax.axis_index("zh")) * (Y * CORE)
    pick = tiles_held()[None, :] == lax.broadcasted_iota(jnp.int32, (Y * CORE, 1), 0)
    listed = lax.dynamic_slice_in_dim(tile_mask, start, Y * CORE, 1).astype(jnp.float32)
    listed = listed.reshape(ZL, X, Y * CORE).transpose(1, 0, 2).reshape(X * ZL, Y * CORE)
    pick = jnp.repeat(pick.astype(jnp.float32), tile_lands, axis=1)
    listed = jnp.dot(listed, pick, preferred_element_type=jnp.float32)

    pair = jnp.concatenate([mine, swap_cores(mine)], axis=0)
    first = send_on(pair, 1)
    third = send_on(pair, 3)
    fourth = send_on(mine, 4)
    first, listed = lax.optimization_barrier((first, listed))
    second = send_on(first, 1)
    own = jnp.zeros((Y * tile_lands, width + classes), jnp.bfloat16)
    for place, tiles in ((0, mine), (1, first), (3, second), (5, third), (7, fourth)):
        own = lax.dynamic_update_slice_in_dim(own, tiles, place * tile_lands, 0)
    other = swap_cores(own)
    gathered = gather_direct(gathered, "x", X)

    own_f = own[:, :width].astype(jnp.float32)
    half_norm = 0.5 * jnp.sum(own_f * own_f, axis=1)
    listed = listed.reshape(X * ZL // 8, 8, Y * tile_lands) > 0.5
    own_bias = jnp.where(listed, -scale * half_norm[None, None, :], jnp.float32(UNLISTED))
    other_bias = swap_cores(own_bias)

    parts = score(gathered, own, other, own_bias, other_bias, width, ZH * rows, rows, scale)
    parts = lax.all_to_all(parts, ("x",) + Z_AXES, 0, 0, tiled=True)
    return merge(parts, rows)


def solution(mesh):
    physical = Mesh(mesh.devices.reshape(ZL, X, ZH, Y, CORE), NAMES)
    split = P(NAMES, None)

    return jax.shard_map(
        local, mesh=physical, in_specs=(split, split, split, P()), out_specs=split, check_vma=False
    )
```

```python
import math

import jax
import jax.numpy as jnp
from jax import lax
from jax.experimental import pallas as pl
from jax.experimental.pallas import tpu as pltpu
from jax.sharding import Mesh, PartitionSpec as P


ZL, X, ZH, Y, CORE = 6, 4, 2, 8, 2
NAMES = ("zl", "x", "zh", "y", "c")
Z_AXES = ("zl", "zh")
Z = ZL * ZH
UNLISTED = -1e30
LANES = 128
VMEM = pl.BlockSpec(memory_space=pltpu.VMEM)


def gather_direct(value, axes, count):
    copies = jnp.broadcast_to(value[None], (count,) + value.shape)
    gathered = lax.all_to_all(copies, axes, 0, 0, tiled=True)
    return gathered.reshape((count * value.shape[0],) + value.shape[1:])


def send_on(tiles, chips):
    pairs = []
    for y in range(Y):
        for core in range(CORE):
            to = (y + (chips if core == 0 else -chips)) % Y
            pairs.append((y * CORE + core, to * CORE + core))
    return lax.ppermute(tiles, ("y", "c"), pairs)


def swap_cores(value):
    return lax.ppermute(value, "c", [(0, 1), (1, 0)])


def tiles_held():
    core = lax.axis_index("c")
    place = lax.broadcasted_iota(jnp.int32, (Y,), 0)
    steps = (place + 1) // 2
    steps = jnp.where(steps == 3, Y - 3, steps)
    flip = jnp.where(place == 0, 0, 1 - place % 2)
    y = (lax.axis_index("y") + jnp.where(core == 0, Y - steps, steps)) % Y
    return y * CORE + (core ^ flip)


def split3(value):
    high = value.astype(jnp.bfloat16)
    rest = value - high.astype(jnp.float32)
    middle = rest.astype(jnp.bfloat16)
    low = (rest - middle.astype(jnp.float32)).astype(jnp.bfloat16)
    return high, middle, low


def stats_rows(row_max, weight_sum, dests, rows):
    lane = lax.broadcasted_iota(jnp.int32, (dests * rows, LANES), 1)
    row = lax.broadcasted_iota(jnp.int32, (dests * rows, LANES), 0) % rows
    stats = jnp.zeros((dests * rows, LANES), jnp.float32)
    for place, piece in enumerate(split3(row_max) + split3(weight_sum)):
        stats = jnp.where(lane // rows == place, piece.astype(jnp.float32), stats)
    stats = jnp.where(lane % rows == row, stats, 0.0)
    return jnp.sum(stats.reshape(dests, rows, LANES), axis=1, keepdims=True)


def score_kernel(
    queries_ref, own_ref, other_ref, own_bias_ref, other_bias_ref, out_ref, *, width, tile_rows, part_rows, scale
):
    rows = queries_ref.shape[0]
    lands = own_ref.shape[0]
    tiles = own_bias_ref.shape[1]
    chunk = tiles * tile_rows

    def step(index):
        start = pl.multiple_of(index * chunk, chunk)
        queries = queries_ref[pl.ds(start, chunk), :]

        def logits_of(land_ref, bias_ref):
            logits = lax.dot_general(
                queries,
                land_ref[:, :width],
                (((1,), (1,)), ((), ())),
                preferred_element_type=jnp.float32,
            )
            logits = (logits * scale).reshape(tiles, tile_rows, lands)
            return (logits + bias_ref[index][:, None, :]).reshape(chunk, lands)

        own = logits_of(own_ref, own_bias_ref)
        other = logits_of(other_ref, other_bias_ref)
        row_max = jnp.max(jnp.maximum(own, other), axis=1, keepdims=True)
        own = jnp.exp(own - row_max)
        other = jnp.exp(other - row_max)
        weight_sum = jnp.sum(own + other, axis=1, keepdims=True)
        label_sum = jnp.dot(
            own.astype(jnp.bfloat16), own_ref[:, width:], preferred_element_type=jnp.float32
        ) + jnp.dot(
            other.astype(jnp.bfloat16), other_ref[:, width:], preferred_element_type=jnp.float32
        )
        dests = chunk // part_rows
        place = pl.ds(pl.multiple_of(index * dests, dests), dests)
        scores = (label_sum / weight_sum).astype(jnp.bfloat16)
        out_ref[place, :part_rows, :] = scores.reshape(dests, part_rows, LANES)
        stats = stats_rows(row_max, weight_sum, dests, part_rows)
        out_ref[place, part_rows:, :] = jnp.broadcast_to(stats, (dests, 8, LANES)).astype(jnp.bfloat16)

    pl.loop(0, rows // chunk)(step)


def score(queries, own, other, own_bias, other_bias, width, tile_rows, part_rows, scale):
    rows = queries.shape[0]
    lands = own.shape[0] + other.shape[0]
    classes = own.shape[1] - width
    return pl.pallas_call(
        lambda *refs: score_kernel(
            *refs, width=width, tile_rows=tile_rows, part_rows=part_rows, scale=scale
        ),
        out_shape=jax.ShapeDtypeStruct((rows // part_rows, part_rows + 8, classes), jnp.bfloat16),
        in_specs=[VMEM] * 5,
        out_specs=VMEM,
        cost_estimate=pl.CostEstimate(
            flops=2 * rows * lands * (width + classes),
            bytes_accessed=2 * (rows * width + lands * (width + classes) + rows * 192),
            transcendentals=rows * lands,
        ),
        compiler_params=pltpu.CompilerParams(vmem_limit_bytes=24 << 20),
        name="score",
    )(queries, own, other, own_bias, other_bias)


def merge_kernel(parts_ref, out_ref):
    sources = parts_ref.shape[0]
    rows = out_ref.shape[0]
    lane = lax.broadcasted_iota(jnp.int32, (1, rows, LANES), 2)
    row = lax.broadcasted_iota(jnp.int32, (1, rows, LANES), 1)
    stats = parts_ref[:, rows:, :].astype(jnp.float32)
    stats = jnp.concatenate([stats] * (rows // 8), axis=1)
    stats = jnp.where(lane % rows == row, stats, 0.0).astype(jnp.bfloat16)
    piece = lax.broadcasted_iota(jnp.int32, (LANES, 2 * LANES), 0) // rows
    half = lax.broadcasted_iota(jnp.int32, (LANES, 2 * LANES), 1) // LANES
    spread = jnp.where(piece // 3 == half, 1.0, 0.0).astype(jnp.bfloat16)
    stats = jnp.dot(
        stats.reshape(sources * rows, LANES), spread, preferred_element_type=jnp.float32
    ).reshape(sources, rows, 2 * LANES)
    row_max = stats[:, :, :LANES]
    weight = stats[:, :, LANES:] * jnp.exp(row_max - jnp.max(row_max, axis=0, keepdims=True))
    labels = jnp.sum(parts_ref[:, :rows, :].astype(jnp.float32) * weight, axis=0)
    out_ref[...] = (labels / jnp.sum(weight, axis=0)).astype(jnp.bfloat16)


def merge(parts, rows):
    return pl.pallas_call(
        merge_kernel,
        out_shape=jax.ShapeDtypeStruct((rows, parts.shape[2]), jnp.bfloat16),
        in_specs=[VMEM],
        out_specs=VMEM,
        compiler_params=pltpu.CompilerParams(vmem_limit_bytes=8 << 20),
        name="merge",
    )(parts)


def local(queries, landmarks, labels, tile_mask):
    rows, width = queries.shape
    tile_lands, classes = labels.shape
    scale = 4.0 / math.sqrt(width)
    mine = jnp.concatenate([landmarks, labels], axis=1)
    gathered = gather_direct(queries, Z_AXES, Z)
    place = lax.axis_index("zl") * X + lax.axis_index("x")
    start = (place * ZH + lax.axis_index("zh")) * (Y * CORE)
    pick = tiles_held()[None, :] == lax.broadcasted_iota(jnp.int32, (Y * CORE, 1), 0)
    listed = lax.dynamic_slice_in_dim(tile_mask, start, Y * CORE, 1).astype(jnp.float32)
    listed = listed.reshape(ZL, X, Y * CORE).transpose(1, 0, 2).reshape(X * ZL, Y * CORE)
    pick = jnp.repeat(pick.astype(jnp.float32), tile_lands, axis=1)
    listed = jnp.dot(listed, pick, preferred_element_type=jnp.float32)

    pair = jnp.concatenate([mine, swap_cores(mine)], axis=0)
    third = send_on(pair, -3)
    first = send_on(pair, 1)
    second = send_on(pair, 2)
    fourth = send_on(mine, 4)
    fourth, listed = lax.optimization_barrier((fourth, listed))
    own = jnp.zeros((Y * tile_lands, width + classes), jnp.bfloat16)
    for place, tiles in ((0, mine), (5, third), (1, first), (3, second), (7, fourth)):
        own = lax.dynamic_update_slice_in_dim(own, tiles, place * tile_lands, 0)
    other = swap_cores(own)
    gathered = gather_direct(gathered, "x", X)

    own_f = own[:, :width].astype(jnp.float32)
    half_norm = 0.5 * jnp.sum(own_f * own_f, axis=1)
    listed = listed.reshape(X * ZL // 8, 8, Y * tile_lands) > 0.5
    own_bias = jnp.where(listed, -scale * half_norm[None, None, :], jnp.float32(UNLISTED))
    other_bias = swap_cores(own_bias)

    parts = score(gathered, own, other, own_bias, other_bias, width, ZH * rows, rows, scale)
    parts = lax.all_to_all(parts, ("x",) + Z_AXES, 0, 0, tiled=True)
    return merge(parts, rows)


def solution(mesh):
    physical = Mesh(mesh.devices.reshape(ZL, X, ZH, Y, CORE), NAMES)
    split = P(NAMES, None)

    return jax.shard_map(
        local, mesh=physical, in_specs=(split, split, split, P()), out_specs=split, check_vma=False
    )
```

```python
import math

import jax
import jax.numpy as jnp
from jax import lax
from jax.experimental import pallas as pl
from jax.experimental.pallas import tpu as pltpu
from jax.sharding import Mesh, PartitionSpec as P


ZL, X, ZH, Y, CORE = 6, 4, 2, 8, 2
NAMES = ("zl", "x", "zh", "y", "c")
Z_AXES = ("zl", "zh")
Z = ZL * ZH
UNLISTED = -1e30
LANES = 128
VMEM = pl.BlockSpec(memory_space=pltpu.VMEM)


def gather_direct(value, axes, count):
    copies = jnp.broadcast_to(value[None], (count,) + value.shape)
    gathered = lax.all_to_all(copies, axes, 0, 0, tiled=True)
    return gathered.reshape((count * value.shape[0],) + value.shape[1:])


def send_on(tiles, chips):
    pairs = []
    for y in range(Y):
        for core in range(CORE):
            to = (y + (chips if core == 0 else -chips)) % Y
            pairs.append((y * CORE + core, to * CORE + core))
    return lax.ppermute(tiles, ("y", "c"), pairs)


def swap_cores(value):
    return lax.ppermute(value, "c", [(0, 1), (1, 0)])


def tiles_held():
    y, core = lax.axis_index("y"), lax.axis_index("c")
    place = lax.broadcasted_iota(jnp.int32, (Y,), 0)
    pair = (place + 1) // 2
    steps = jnp.where(pair == 1, 2, jnp.where(pair == 2, Y - 3, jnp.where(pair == 3, 1, pair)))
    flip = jnp.where(place == 0, 0, 1 - place % 2)

    def of(core):
        return (y + jnp.where(core == 0, Y - steps, steps)) % Y * CORE + (core ^ flip)

    return jnp.concatenate([of(core), of(1 - core)])


def split3(value):
    high = value.astype(jnp.bfloat16)
    rest = value - high.astype(jnp.float32)
    middle = rest.astype(jnp.bfloat16)
    low = (rest - middle.astype(jnp.float32)).astype(jnp.bfloat16)
    return high, middle, low


def stats_rows(row_max, weight_sum, dests, rows):
    lane = lax.broadcasted_iota(jnp.int32, (dests * rows, LANES), 1)
    row = lax.broadcasted_iota(jnp.int32, (dests * rows, LANES), 0) % rows
    stats = jnp.zeros((dests * rows, LANES), jnp.float32)
    for place, piece in enumerate(split3(row_max) + split3(weight_sum)):
        stats = jnp.where(lane // rows == place, piece.astype(jnp.float32), stats)
    stats = jnp.where(lane % rows == row, stats, 0.0)
    return jnp.sum(stats.reshape(dests, rows, LANES), axis=1, keepdims=True)


def score_kernel(queries_ref, *refs, width, tile_rows, part_rows, scale):
    *piece_refs, bias_ref, out_ref, land_ref = refs
    lands = land_ref.shape[0]
    tiles = bias_ref.shape[1]
    chunk = tiles * tile_rows
    dests = chunk // part_rows
    first = 0
    for piece_ref in piece_refs:
        land_ref[first : first + piece_ref.shape[0], :] = piece_ref[...]
        first += piece_ref.shape[0]

    def step(index):
        start = pl.multiple_of(index * chunk, chunk)
        logits = lax.dot_general(
            queries_ref[pl.ds(start, chunk), :],
            land_ref[:, :width],
            (((1,), (1,)), ((), ())),
            preferred_element_type=jnp.float32,
        )
        logits = (logits * scale).reshape(tiles, tile_rows, lands) + bias_ref[index][:, None, :]
        logits = logits.reshape(chunk, lands)
        row_max = jnp.max(logits, axis=1, keepdims=True)
        kernel = jnp.exp(logits - row_max)
        weight_sum = jnp.sum(kernel, axis=1, keepdims=True)
        label_sum = jnp.dot(
            kernel.astype(jnp.bfloat16), land_ref[:, width:], preferred_element_type=jnp.float32
        )
        place = pl.ds(pl.multiple_of(index * dests, dests), dests)
        scores = (label_sum / weight_sum).astype(jnp.bfloat16)
        out_ref[place, :part_rows, :] = scores.reshape(dests, part_rows, LANES)
        stats = stats_rows(row_max, weight_sum, dests, part_rows)
        out_ref[place, part_rows:, :] = jnp.broadcast_to(stats, (dests, 8, LANES)).astype(jnp.bfloat16)

    pl.loop(0, queries_ref.shape[0] // chunk)(step)


def score(queries, pieces, bias, width, tile_rows, part_rows, scale):
    rows = queries.shape[0]
    lands = bias.shape[2]
    classes = pieces[0].shape[1] - width
    return pl.pallas_call(
        lambda *refs: score_kernel(
            *refs, width=width, tile_rows=tile_rows, part_rows=part_rows, scale=scale
        ),
        out_shape=jax.ShapeDtypeStruct((rows // part_rows, part_rows + 8, classes), jnp.bfloat16),
        in_specs=[VMEM] * (len(pieces) + 2),
        out_specs=VMEM,
        scratch_shapes=[pltpu.VMEM((lands, width + classes), jnp.bfloat16)],
        cost_estimate=pl.CostEstimate(
            flops=2 * rows * lands * (width + classes),
            bytes_accessed=2 * (rows * width + lands * (width + classes) + rows * 192),
            transcendentals=rows * lands,
        ),
        compiler_params=pltpu.CompilerParams(vmem_limit_bytes=24 << 20),
        name="score",
    )(queries, *pieces, bias)


def merge_kernel(parts_ref, out_ref):
    sources = parts_ref.shape[0]
    rows = out_ref.shape[0]
    lane = lax.broadcasted_iota(jnp.int32, (1, rows, LANES), 2)
    row = lax.broadcasted_iota(jnp.int32, (1, rows, LANES), 1)
    stats = parts_ref[:, rows:, :].astype(jnp.float32)
    stats = jnp.concatenate([stats] * (rows // 8), axis=1)
    stats = jnp.where(lane % rows == row, stats, 0.0).astype(jnp.bfloat16)
    piece = lax.broadcasted_iota(jnp.int32, (LANES, 2 * LANES), 0) // rows
    half = lax.broadcasted_iota(jnp.int32, (LANES, 2 * LANES), 1) // LANES
    spread = jnp.where(piece // 3 == half, 1.0, 0.0).astype(jnp.bfloat16)
    stats = jnp.dot(
        stats.reshape(sources * rows, LANES), spread, preferred_element_type=jnp.float32
    ).reshape(sources, rows, 2 * LANES)
    row_max = stats[:, :, :LANES]
    weight = stats[:, :, LANES:] * jnp.exp(row_max - jnp.max(row_max, axis=0, keepdims=True))
    labels = jnp.sum(parts_ref[:, :rows, :].astype(jnp.float32) * weight, axis=0)
    out_ref[...] = (labels / jnp.sum(weight, axis=0)).astype(jnp.bfloat16)


def merge(parts, rows):
    return pl.pallas_call(
        merge_kernel,
        out_shape=jax.ShapeDtypeStruct((rows, parts.shape[2]), jnp.bfloat16),
        in_specs=[VMEM],
        out_specs=VMEM,
        compiler_params=pltpu.CompilerParams(vmem_limit_bytes=8 << 20),
        name="merge",
    )(parts)


def local(queries, landmarks, labels, tile_mask):
    rows, width = queries.shape
    tile_lands, _ = labels.shape
    scale = 4.0 / math.sqrt(width)
    mine = jnp.concatenate([landmarks, labels], axis=1)
    gathered = gather_direct(queries, Z_AXES, Z)
    place = lax.axis_index("zl") * X + lax.axis_index("x")
    start = (place * ZH + lax.axis_index("zh")) * (Y * CORE)
    pick = tiles_held()[None, :] == lax.broadcasted_iota(jnp.int32, (Y * CORE, 1), 0)
    listed = lax.dynamic_slice_in_dim(tile_mask, start, Y * CORE, 1).astype(jnp.float32)
    listed = listed.reshape(ZL, X, Y * CORE).transpose(1, 0, 2).reshape(X * ZL, Y * CORE)
    pick = jnp.repeat(pick.astype(jnp.float32), tile_lands, axis=1)
    listed = jnp.dot(listed, pick, preferred_element_type=jnp.float32)

    pair = jnp.concatenate([mine, swap_cores(mine)], axis=0)
    second = send_on(pair, 2)
    third = send_on(pair, -3)
    fourth = send_on(second[:tile_lands], 2)
    first = send_on(pair, 1)
    first, listed = lax.optimization_barrier((first, listed))
    early = jnp.concatenate([mine, second, third], axis=0)
    late = jnp.concatenate([first, fourth], axis=0)
    other_early = swap_cores(early)
    other_late = swap_cores(late)
    gathered = gather_direct(gathered, "x", X)

    def half_norm(land):
        land_f = land[:, :width].astype(jnp.float32)
        return 0.5 * jnp.sum(land_f * land_f, axis=1)

    pieces = (early, late, other_early, other_late)
    norms = jnp.concatenate([half_norm(piece) for piece in pieces])
    listed = listed.reshape(X * ZL // 8, 8, CORE * Y * tile_lands) > 0.5
    bias = jnp.where(listed, -scale * norms[None, None, :], jnp.float32(UNLISTED))

    parts = score(gathered, pieces, bias, width, ZH * rows, rows, scale)
    parts = lax.all_to_all(parts, ("x",) + Z_AXES, 0, 0, tiled=True)
    return merge(parts, rows)


def solution(mesh):
    physical = Mesh(mesh.devices.reshape(ZL, X, ZH, Y, CORE), NAMES)
    split = P(NAMES, None)

    return jax.shard_map(
        local, mesh=physical, in_specs=(split, split, split, P()), out_specs=split, check_vma=False
    )
```

```python
import math

import jax
import jax.numpy as jnp
from jax import lax
from jax.experimental import pallas as pl
from jax.experimental.pallas import tpu as pltpu
from jax.sharding import Mesh, PartitionSpec as P


ZL, X, ZH, Y, CORE = 6, 4, 2, 8, 2
NAMES = ("zl", "x", "zh", "y", "c")
Z_AXES = ("zl", "zh")
Z = ZL * ZH
UNLISTED = -1e30
LANES = 128
VMEM = pl.BlockSpec(memory_space=pltpu.VMEM)


def gather_direct(value, axes, count):
    copies = jnp.broadcast_to(value[None], (count,) + value.shape)
    gathered = lax.all_to_all(copies, axes, 0, 0, tiled=True)
    return gathered.reshape((count * value.shape[0],) + value.shape[1:])


def send_on(tiles, chips):
    pairs = []
    for y in range(Y):
        for core in range(CORE):
            to = (y + (chips if core == 0 else -chips)) % Y
            pairs.append((y * CORE + core, to * CORE + core))
    return lax.ppermute(tiles, ("y", "c"), pairs)


def swap_cores(value):
    return lax.ppermute(value, "c", [(0, 1), (1, 0)])


def tiles_held():
    core = lax.axis_index("c")
    place = lax.broadcasted_iota(jnp.int32, (Y,), 0)
    steps = (place + 1) // 2
    steps = jnp.where(steps == 3, Y - 3, steps)
    flip = jnp.where(place == 0, 0, 1 - place % 2)
    y = (lax.axis_index("y") + jnp.where(core == 0, Y - steps, steps)) % Y
    return y * CORE + (core ^ flip)


def split3(value):
    high = value.astype(jnp.bfloat16)
    rest = value - high.astype(jnp.float32)
    middle = rest.astype(jnp.bfloat16)
    low = (rest - middle.astype(jnp.float32)).astype(jnp.bfloat16)
    return high, middle, low


def stats_rows(row_max, weight_sum, dests, rows):
    lane = lax.broadcasted_iota(jnp.int32, (dests * rows, LANES), 1)
    row = lax.broadcasted_iota(jnp.int32, (dests * rows, LANES), 0) % rows
    stats = jnp.zeros((dests * rows, LANES), jnp.float32)
    for place, piece in enumerate(split3(row_max) + split3(weight_sum)):
        stats = jnp.where(lane // rows == place, piece.astype(jnp.float32), stats)
    stats = jnp.where(lane % rows == row, stats, 0.0)
    return jnp.sum(stats.reshape(dests, rows, LANES), axis=1, keepdims=True)


def score_kernel(
    queries_ref, own_ref, other_ref, own_bias_ref, other_bias_ref, out_ref, land_ref, *, width, tile_rows, part_rows, scale
):
    lands = land_ref.shape[0]
    tiles = own_bias_ref.shape[1]
    chunk = tiles * tile_rows
    dests = chunk // part_rows
    land_ref[: lands // 2, :] = own_ref[...]
    land_ref[lands // 2 :, :] = other_ref[...]

    def step(index):
        start = pl.multiple_of(index * chunk, chunk)
        logits = lax.dot_general(
            queries_ref[pl.ds(start, chunk), :],
            land_ref[:, :width],
            (((1,), (1,)), ((), ())),
            preferred_element_type=jnp.float32,
        )
        bias = jnp.concatenate([own_bias_ref[index], other_bias_ref[index]], axis=1)
        logits = (logits * scale).reshape(tiles, tile_rows, lands) + bias[:, None, :]
        logits = logits.reshape(chunk, lands)
        row_max = jnp.max(logits, axis=1, keepdims=True)
        kernel = jnp.exp(logits - row_max)
        weight_sum = jnp.sum(kernel, axis=1, keepdims=True)
        label_sum = jnp.dot(
            kernel.astype(jnp.bfloat16), land_ref[:, width:], preferred_element_type=jnp.float32
        )
        place = pl.ds(pl.multiple_of(index * dests, dests), dests)
        scores = (label_sum / weight_sum).astype(jnp.bfloat16)
        out_ref[place, :part_rows, :] = scores.reshape(dests, part_rows, LANES)
        stats = stats_rows(row_max, weight_sum, dests, part_rows)
        out_ref[place, part_rows:, :] = jnp.broadcast_to(stats, (dests, 8, LANES)).astype(jnp.bfloat16)

    pl.loop(0, queries_ref.shape[0] // chunk)(step)


def score(queries, own, other, own_bias, other_bias, width, tile_rows, part_rows, scale):
    rows = queries.shape[0]
    lands = own.shape[0] + other.shape[0]
    classes = own.shape[1] - width
    return pl.pallas_call(
        lambda *refs: score_kernel(
            *refs, width=width, tile_rows=tile_rows, part_rows=part_rows, scale=scale
        ),
        out_shape=jax.ShapeDtypeStruct((rows // part_rows, part_rows + 8, classes), jnp.bfloat16),
        in_specs=[VMEM] * 5,
        out_specs=VMEM,
        scratch_shapes=[pltpu.VMEM((lands, width + classes), jnp.bfloat16)],
        cost_estimate=pl.CostEstimate(
            flops=2 * rows * lands * (width + classes),
            bytes_accessed=2 * (rows * width + lands * (width + classes) + rows * 192),
            transcendentals=rows * lands,
        ),
        compiler_params=pltpu.CompilerParams(vmem_limit_bytes=20 << 20),
        name="score",
    )(queries, own, other, own_bias, other_bias)


def merge_kernel(parts_ref, out_ref):
    sources = parts_ref.shape[0]
    rows = out_ref.shape[0]
    lane = lax.broadcasted_iota(jnp.int32, (1, rows, LANES), 2)
    row = lax.broadcasted_iota(jnp.int32, (1, rows, LANES), 1)
    stats = parts_ref[:, rows:, :].astype(jnp.float32)
    stats = jnp.concatenate([stats] * (rows // 8), axis=1)
    stats = jnp.where(lane % rows == row, stats, 0.0).astype(jnp.bfloat16)
    piece = lax.broadcasted_iota(jnp.int32, (LANES, 2 * LANES), 0) // rows
    half = lax.broadcasted_iota(jnp.int32, (LANES, 2 * LANES), 1) // LANES
    spread = jnp.where(piece // 3 == half, 1.0, 0.0).astype(jnp.bfloat16)
    stats = jnp.dot(
        stats.reshape(sources * rows, LANES), spread, preferred_element_type=jnp.float32
    ).reshape(sources, rows, 2 * LANES)
    row_max = stats[:, :, :LANES]
    weight = stats[:, :, LANES:] * jnp.exp(row_max - jnp.max(row_max, axis=0, keepdims=True))
    labels = jnp.sum(parts_ref[:, :rows, :].astype(jnp.float32) * weight, axis=0)
    out_ref[...] = (labels / jnp.sum(weight, axis=0)).astype(jnp.bfloat16)


def merge(parts, rows):
    return pl.pallas_call(
        merge_kernel,
        out_shape=jax.ShapeDtypeStruct((rows, parts.shape[2]), jnp.bfloat16),
        in_specs=[VMEM],
        out_specs=VMEM,
        compiler_params=pltpu.CompilerParams(vmem_limit_bytes=8 << 20),
        name="merge",
    )(parts)


def local(queries, landmarks, labels, tile_mask):
    rows, width = queries.shape
    tile_lands, classes = labels.shape
    scale = 4.0 / math.sqrt(width)
    mine = jnp.concatenate([landmarks, labels], axis=1)
    gathered = gather_direct(queries, Z_AXES, Z)
    place = lax.axis_index("zl") * X + lax.axis_index("x")
    start = (place * ZH + lax.axis_index("zh")) * (Y * CORE)
    pick = tiles_held()[None, :] == lax.broadcasted_iota(jnp.int32, (Y * CORE, 1), 0)
    listed = lax.dynamic_slice_in_dim(tile_mask, start, Y * CORE, 1).astype(jnp.float32)
    listed = listed.reshape(ZL, X, Y * CORE).transpose(1, 0, 2).reshape(X * ZL, Y * CORE)
    pick = jnp.repeat(pick.astype(jnp.float32), tile_lands, axis=1)
    listed = jnp.dot(listed, pick, preferred_element_type=jnp.float32)

    pair = jnp.concatenate([mine, swap_cores(mine)], axis=0)
    third = send_on(pair, -3)
    first = send_on(pair, 1)
    second = send_on(pair, 2)
    fourth = send_on(second[:tile_lands], 2)
    fourth, listed = lax.optimization_barrier((fourth, listed))
    own = jnp.zeros((Y * tile_lands, width + classes), jnp.bfloat16)
    for place, tiles in ((0, mine), (3, second), (5, third), (1, first), (7, fourth)):
        own = lax.dynamic_update_slice_in_dim(own, tiles, place * tile_lands, 0)
    other = swap_cores(own)
    gathered = gather_direct(gathered, "x", X)

    own_f = own[:, :width].astype(jnp.float32)
    half_norm = 0.5 * jnp.sum(own_f * own_f, axis=1)
    listed = listed.reshape(X * ZL // 8, 8, Y * tile_lands) > 0.5
    own_bias = jnp.where(listed, -scale * half_norm[None, None, :], jnp.float32(UNLISTED))
    other_bias = swap_cores(own_bias)

    parts = score(gathered, own, other, own_bias, other_bias, width, ZH * rows, rows, scale)
    parts = lax.all_to_all(parts, ("x",) + Z_AXES, 0, 0, tiled=True)
    return merge(parts, rows)


def solution(mesh):
    physical = Mesh(mesh.devices.reshape(ZL, X, ZH, Y, CORE), NAMES)
    split = P(NAMES, None)

    return jax.shard_map(
        local, mesh=physical, in_specs=(split, split, split, P()), out_specs=split, check_vma=False
    )
```

```python
import math

import jax
import jax.numpy as jnp
from jax import lax
from jax.experimental import pallas as pl
from jax.experimental.pallas import tpu as pltpu
from jax.sharding import Mesh, PartitionSpec as P


ZL, X, ZH, Y, CORE = 6, 4, 2, 8, 2
NAMES = ("zl", "x", "zh", "y", "c")
Z_AXES = ("zl", "zh")
Z = ZL * ZH
UNLISTED = -1e30
LANES = 128
VMEM = pl.BlockSpec(memory_space=pltpu.VMEM)
ANYWHERE = pl.BlockSpec(memory_space=pl.ANY)


def gather_direct(value, axes, count):
    copies = jnp.broadcast_to(value[None], (count,) + value.shape)
    gathered = lax.all_to_all(copies, axes, 0, 0, tiled=True)
    return gathered.reshape((count * value.shape[0],) + value.shape[1:])


def send_on(tiles, chips):
    pairs = []
    for y in range(Y):
        for core in range(CORE):
            to = (y + (chips if core == 0 else -chips)) % Y
            pairs.append((y * CORE + core, to * CORE + core))
    return lax.ppermute(tiles, ("y", "c"), pairs)


def swap_cores(value):
    return lax.ppermute(value, "c", [(0, 1), (1, 0)])


def tiles_held():
    core = lax.axis_index("c")
    place = lax.broadcasted_iota(jnp.int32, (Y,), 0)
    steps = (place + 1) // 2
    steps = jnp.where(steps == 3, Y - 3, steps)
    flip = jnp.where(place == 0, 0, 1 - place % 2)
    y = (lax.axis_index("y") + jnp.where(core == 0, Y - steps, steps)) % Y
    return y * CORE + (core ^ flip)


def split3(value):
    high = value.astype(jnp.bfloat16)
    rest = value - high.astype(jnp.float32)
    middle = rest.astype(jnp.bfloat16)
    low = (rest - middle.astype(jnp.float32)).astype(jnp.bfloat16)
    return high, middle, low


def stats_rows(row_max, weight_sum, dests, rows):
    lane = lax.broadcasted_iota(jnp.int32, (dests * rows, LANES), 1)
    row = lax.broadcasted_iota(jnp.int32, (dests * rows, LANES), 0) % rows
    stats = jnp.zeros((dests * rows, LANES), jnp.float32)
    for place, piece in enumerate(split3(row_max) + split3(weight_sum)):
        stats = jnp.where(lane // rows == place, piece.astype(jnp.float32), stats)
    stats = jnp.where(lane % rows == row, stats, 0.0)
    return jnp.sum(stats.reshape(dests, rows, LANES), axis=1, keepdims=True)


def score_kernel(
    queries_ref, own_ref, other_ref, own_bias_ref, other_bias_ref, out_ref, land_ref, sems, *, width, tile_rows, part_rows, scale
):
    lands = land_ref.shape[0]
    tiles = own_bias_ref.shape[1]
    chunk = tiles * tile_rows
    dests = chunk // part_rows
    copies = [
        pltpu.make_async_copy(piece, land_ref.at[pl.ds(half * (lands // 2), lands // 2), :], sems.at[half])
        for half, piece in enumerate((own_ref, other_ref))
    ]
    for copy in copies:
        copy.start()
    for copy in copies:
        copy.wait()

    def step(index):
        start = pl.multiple_of(index * chunk, chunk)
        logits = lax.dot_general(
            queries_ref[pl.ds(start, chunk), :],
            land_ref[:, :width],
            (((1,), (1,)), ((), ())),
            preferred_element_type=jnp.float32,
        )
        bias = jnp.concatenate([own_bias_ref[index], other_bias_ref[index]], axis=1)
        logits = (logits * scale).reshape(tiles, tile_rows, lands) + bias[:, None, :]
        logits = logits.reshape(chunk, lands)
        row_max = jnp.max(logits, axis=1, keepdims=True)
        kernel = jnp.exp(logits - row_max)
        weight_sum = jnp.sum(kernel, axis=1, keepdims=True)
        label_sum = jnp.dot(
            kernel.astype(jnp.bfloat16), land_ref[:, width:], preferred_element_type=jnp.float32
        )
        place = pl.ds(pl.multiple_of(index * dests, dests), dests)
        scores = (label_sum / weight_sum).astype(jnp.bfloat16)
        out_ref[place, :part_rows, :] = scores.reshape(dests, part_rows, LANES)
        stats = stats_rows(row_max, weight_sum, dests, part_rows)
        out_ref[place, part_rows:, :] = jnp.broadcast_to(stats, (dests, 8, LANES)).astype(jnp.bfloat16)

    pl.loop(0, queries_ref.shape[0] // chunk)(step)


def score(queries, own, other, own_bias, other_bias, width, tile_rows, part_rows, scale):
    rows = queries.shape[0]
    lands = own.shape[0] + other.shape[0]
    classes = own.shape[1] - width
    return pl.pallas_call(
        lambda *refs: score_kernel(
            *refs, width=width, tile_rows=tile_rows, part_rows=part_rows, scale=scale
        ),
        out_shape=jax.ShapeDtypeStruct((rows // part_rows, part_rows + 8, classes), jnp.bfloat16),
        in_specs=[VMEM, ANYWHERE, ANYWHERE, VMEM, VMEM],
        out_specs=VMEM,
        scratch_shapes=[
            pltpu.VMEM((lands, width + classes), jnp.bfloat16),
            pltpu.SemaphoreType.DMA((2,)),
        ],
        cost_estimate=pl.CostEstimate(
            flops=2 * rows * lands * (width + classes),
            bytes_accessed=2 * (rows * width + lands * (width + classes) + rows * 192),
            transcendentals=rows * lands,
        ),
        compiler_params=pltpu.CompilerParams(vmem_limit_bytes=20 << 20),
        name="score",
    )(queries, own, other, own_bias, other_bias)


def merge_kernel(parts_ref, out_ref):
    sources = parts_ref.shape[0]
    rows = out_ref.shape[0]
    lane = lax.broadcasted_iota(jnp.int32, (1, rows, LANES), 2)
    row = lax.broadcasted_iota(jnp.int32, (1, rows, LANES), 1)
    stats = parts_ref[:, rows:, :].astype(jnp.float32)
    stats = jnp.concatenate([stats] * (rows // 8), axis=1)
    stats = jnp.where(lane % rows == row, stats, 0.0).astype(jnp.bfloat16)
    piece = lax.broadcasted_iota(jnp.int32, (LANES, 2 * LANES), 0) // rows
    half = lax.broadcasted_iota(jnp.int32, (LANES, 2 * LANES), 1) // LANES
    spread = jnp.where(piece // 3 == half, 1.0, 0.0).astype(jnp.bfloat16)
    stats = jnp.dot(
        stats.reshape(sources * rows, LANES), spread, preferred_element_type=jnp.float32
    ).reshape(sources, rows, 2 * LANES)
    row_max = stats[:, :, :LANES]
    weight = stats[:, :, LANES:] * jnp.exp(row_max - jnp.max(row_max, axis=0, keepdims=True))
    labels = jnp.sum(parts_ref[:, :rows, :].astype(jnp.float32) * weight, axis=0)
    out_ref[...] = (labels / jnp.sum(weight, axis=0)).astype(jnp.bfloat16)


def merge(parts, rows):
    return pl.pallas_call(
        merge_kernel,
        out_shape=jax.ShapeDtypeStruct((rows, parts.shape[2]), jnp.bfloat16),
        in_specs=[VMEM],
        out_specs=VMEM,
        compiler_params=pltpu.CompilerParams(vmem_limit_bytes=8 << 20),
        name="merge",
    )(parts)


def local(queries, landmarks, labels, tile_mask):
    rows, width = queries.shape
    tile_lands, classes = labels.shape
    scale = 4.0 / math.sqrt(width)
    mine = jnp.concatenate([landmarks, labels], axis=1)
    gathered = gather_direct(queries, Z_AXES, Z)
    place = lax.axis_index("zl") * X + lax.axis_index("x")
    start = (place * ZH + lax.axis_index("zh")) * (Y * CORE)
    pick = tiles_held()[None, :] == lax.broadcasted_iota(jnp.int32, (Y * CORE, 1), 0)
    listed = lax.dynamic_slice_in_dim(tile_mask, start, Y * CORE, 1).astype(jnp.float32)
    listed = listed.reshape(ZL, X, Y * CORE).transpose(1, 0, 2).reshape(X * ZL, Y * CORE)
    pick = jnp.repeat(pick.astype(jnp.float32), tile_lands, axis=1)
    listed = jnp.dot(listed, pick, preferred_element_type=jnp.float32)

    pair = jnp.concatenate([mine, swap_cores(mine)], axis=0)
    third = send_on(pair, -3)
    first = send_on(pair, 1)
    second = send_on(pair, 2)
    fourth = send_on(second[:tile_lands], 2)
    first, listed = lax.optimization_barrier((first, listed))
    own = jnp.zeros((Y * tile_lands, width + classes), jnp.bfloat16)
    for place, tiles in ((0, mine), (3, second), (5, third), (7, fourth), (1, first)):
        own = lax.dynamic_update_slice_in_dim(own, tiles, place * tile_lands, 0)
    other = swap_cores(own)
    gathered = gather_direct(gathered, "x", X)

    own_f = own[:, :width].astype(jnp.float32)
    half_norm = 0.5 * jnp.sum(own_f * own_f, axis=1)
    listed = listed.reshape(X * ZL // 8, 8, Y * tile_lands) > 0.5
    own_bias = jnp.where(listed, -scale * half_norm[None, None, :], jnp.float32(UNLISTED))
    other_bias = swap_cores(own_bias)

    parts = score(gathered, own, other, own_bias, other_bias, width, ZH * rows, rows, scale)
    parts = lax.all_to_all(parts, ("x",) + Z_AXES, 0, 0, tiled=True)
    return merge(parts, rows)


def solution(mesh):
    physical = Mesh(mesh.devices.reshape(ZL, X, ZH, Y, CORE), NAMES)
    split = P(NAMES, None)

    return jax.shard_map(
        local, mesh=physical, in_specs=(split, split, split, P()), out_specs=split, check_vma=False
    )
```

```python
import math

import jax
import jax.numpy as jnp
from jax import lax
from jax.experimental import pallas as pl
from jax.experimental.pallas import tpu as pltpu
from jax.sharding import Mesh, PartitionSpec as P


ZL, X, ZH, Y, CORE = 6, 4, 2, 8, 2
NAMES = ("zl", "x", "zh", "y", "c")
Z_AXES = ("zl", "zh")
Z = ZL * ZH
UNLISTED = -1e30
LANES = 128
VMEM = pl.BlockSpec(memory_space=pltpu.VMEM)


def gather_direct(value, axes, count):
    copies = jnp.broadcast_to(value[None], (count,) + value.shape)
    gathered = lax.all_to_all(copies, axes, 0, 0, tiled=True)
    return gathered.reshape((count * value.shape[0],) + value.shape[1:])


def send_on(tiles, chips):
    pairs = []
    for y in range(Y):
        for core in range(CORE):
            to = (y + (chips if core == 0 else -chips)) % Y
            pairs.append((y * CORE + core, to * CORE + core))
    return lax.ppermute(tiles, ("y", "c"), pairs)


def swap_cores(value):
    return lax.ppermute(value, "c", [(0, 1), (1, 0)])


def tiles_held():
    core = lax.axis_index("c")
    place = lax.broadcasted_iota(jnp.int32, (Y,), 0)
    steps = (place + 1) // 2
    steps = jnp.where(steps == 3, Y - 3, steps)
    flip = jnp.where(place == 0, 0, 1 - place % 2)
    y = (lax.axis_index("y") + jnp.where(core == 0, Y - steps, steps)) % Y
    return y * CORE + (core ^ flip)


def split3(value):
    high = value.astype(jnp.bfloat16)
    rest = value - high.astype(jnp.float32)
    middle = rest.astype(jnp.bfloat16)
    low = (rest - middle.astype(jnp.float32)).astype(jnp.bfloat16)
    return high, middle, low


def stats_rows(row_max, weight_sum, dests, rows):
    lane = lax.broadcasted_iota(jnp.int32, (dests * rows, LANES), 1)
    row = lax.broadcasted_iota(jnp.int32, (dests * rows, LANES), 0) % rows
    stats = jnp.zeros((dests * rows, LANES), jnp.float32)
    for place, piece in enumerate(split3(row_max) + split3(weight_sum)):
        stats = jnp.where(lane // rows == place, piece.astype(jnp.float32), stats)
    stats = jnp.where(lane % rows == row, stats, 0.0)
    return jnp.sum(stats.reshape(dests, rows, LANES), axis=1, keepdims=True)


def score_kernel(
    queries_ref, own_ref, other_ref, own_bias_ref, other_bias_ref, out_ref, *, width, tile_rows, part_rows, scale
):
    rows = queries_ref.shape[0]
    lands = own_ref.shape[0]
    tiles = own_bias_ref.shape[1]
    chunk = tiles * tile_rows

    def step(index):
        start = pl.multiple_of(index * chunk, chunk)
        queries = queries_ref[pl.ds(start, chunk), :]

        def logits_of(land_ref, bias_ref):
            logits = lax.dot_general(
                queries,
                land_ref[:, :width],
                (((1,), (1,)), ((), ())),
                preferred_element_type=jnp.float32,
            )
            logits = (logits * scale).reshape(tiles, tile_rows, lands)
            return (logits + bias_ref[index][:, None, :]).reshape(chunk, lands)

        own = logits_of(own_ref, own_bias_ref)
        other = logits_of(other_ref, other_bias_ref)
        row_max = jnp.max(jnp.maximum(own, other), axis=1, keepdims=True)
        own = jnp.exp(own - row_max)
        other = jnp.exp(other - row_max)
        weight_sum = jnp.sum(own + other, axis=1, keepdims=True)
        label_sum = jnp.dot(
            own.astype(jnp.bfloat16), own_ref[:, width:], preferred_element_type=jnp.float32
        ) + jnp.dot(
            other.astype(jnp.bfloat16), other_ref[:, width:], preferred_element_type=jnp.float32
        )
        dests = chunk // part_rows
        place = pl.ds(pl.multiple_of(index * dests, dests), dests)
        scores = (label_sum / weight_sum).astype(jnp.bfloat16)
        out_ref[place, :part_rows, :] = scores.reshape(dests, part_rows, LANES)
        stats = stats_rows(row_max, weight_sum, dests, part_rows)
        out_ref[place, part_rows:, :] = jnp.broadcast_to(stats, (dests, 8, LANES)).astype(jnp.bfloat16)

    pl.loop(0, rows // chunk, unroll=True)(step)


def score(queries, own, other, own_bias, other_bias, width, tile_rows, part_rows, scale):
    rows = queries.shape[0]
    lands = own.shape[0] + other.shape[0]
    classes = own.shape[1] - width
    return pl.pallas_call(
        lambda *refs: score_kernel(
            *refs, width=width, tile_rows=tile_rows, part_rows=part_rows, scale=scale
        ),
        out_shape=jax.ShapeDtypeStruct((rows // part_rows, part_rows + 8, classes), jnp.bfloat16),
        in_specs=[VMEM] * 5,
        out_specs=VMEM,
        cost_estimate=pl.CostEstimate(
            flops=2 * rows * lands * (width + classes),
            bytes_accessed=2 * (rows * width + lands * (width + classes) + rows * 192),
            transcendentals=rows * lands,
        ),
        compiler_params=pltpu.CompilerParams(vmem_limit_bytes=24 << 20),
        name="score",
    )(queries, own, other, own_bias, other_bias)


def merge_kernel(parts_ref, out_ref):
    sources = parts_ref.shape[0]
    rows = out_ref.shape[0]
    lane = lax.broadcasted_iota(jnp.int32, (1, rows, LANES), 2)
    row = lax.broadcasted_iota(jnp.int32, (1, rows, LANES), 1)
    stats = parts_ref[:, rows:, :].astype(jnp.float32)
    stats = jnp.concatenate([stats] * (rows // 8), axis=1)
    stats = jnp.where(lane % rows == row, stats, 0.0).astype(jnp.bfloat16)
    piece = lax.broadcasted_iota(jnp.int32, (LANES, 2 * LANES), 0) // rows
    half = lax.broadcasted_iota(jnp.int32, (LANES, 2 * LANES), 1) // LANES
    spread = jnp.where(piece // 3 == half, 1.0, 0.0).astype(jnp.bfloat16)
    stats = jnp.dot(
        stats.reshape(sources * rows, LANES), spread, preferred_element_type=jnp.float32
    ).reshape(sources, rows, 2 * LANES)
    row_max = stats[:, :, :LANES]
    weight = stats[:, :, LANES:] * jnp.exp(row_max - jnp.max(row_max, axis=0, keepdims=True))
    labels = jnp.sum(parts_ref[:, :rows, :].astype(jnp.float32) * weight, axis=0)
    out_ref[...] = (labels / jnp.sum(weight, axis=0)).astype(jnp.bfloat16)


def merge(parts, rows):
    return pl.pallas_call(
        merge_kernel,
        out_shape=jax.ShapeDtypeStruct((rows, parts.shape[2]), jnp.bfloat16),
        in_specs=[VMEM],
        out_specs=VMEM,
        compiler_params=pltpu.CompilerParams(vmem_limit_bytes=8 << 20),
        name="merge",
    )(parts)


def local(queries, landmarks, labels, tile_mask):
    rows, width = queries.shape
    tile_lands, classes = labels.shape
    scale = 4.0 / math.sqrt(width)
    mine = jnp.concatenate([landmarks, labels], axis=1)
    gathered = gather_direct(queries, Z_AXES, Z)
    place = lax.axis_index("zl") * X + lax.axis_index("x")
    start = (place * ZH + lax.axis_index("zh")) * (Y * CORE)
    pick = tiles_held()[None, :] == lax.broadcasted_iota(jnp.int32, (Y * CORE, 1), 0)
    listed = lax.dynamic_slice_in_dim(tile_mask, start, Y * CORE, 1).astype(jnp.float32)
    listed = listed.reshape(ZL, X, Y * CORE).transpose(1, 0, 2).reshape(X * ZL, Y * CORE)
    pick = jnp.repeat(pick.astype(jnp.float32), tile_lands, axis=1)
    listed = jnp.dot(listed, pick, preferred_element_type=jnp.float32)

    pair = jnp.concatenate([mine, swap_cores(mine)], axis=0)
    third = send_on(pair, -3)
    first = send_on(pair, 1)
    second = send_on(pair, 2)
    fourth = send_on(second[:tile_lands], 2)
    fourth, listed = lax.optimization_barrier((fourth, listed))
    own = jnp.zeros((Y * tile_lands, width + classes), jnp.bfloat16)
    for place, tiles in ((0, mine), (3, second), (5, third), (1, first), (7, fourth)):
        own = lax.dynamic_update_slice_in_dim(own, tiles, place * tile_lands, 0)
    other = swap_cores(own)
    gathered = gather_direct(gathered, "x", X)

    own_f = own[:, :width].astype(jnp.float32)
    half_norm = 0.5 * jnp.sum(own_f * own_f, axis=1)
    listed = listed.reshape(X * ZL // 8, 8, Y * tile_lands) > 0.5
    own_bias = jnp.where(listed, -scale * half_norm[None, None, :], jnp.float32(UNLISTED))
    other_bias = swap_cores(own_bias)

    parts = score(gathered, own, other, own_bias, other_bias, width, ZH * rows, rows, scale)
    parts = lax.all_to_all(parts, ("x",) + Z_AXES, 0, 0, tiled=True)
    return merge(parts, rows)


def solution(mesh):
    physical = Mesh(mesh.devices.reshape(ZL, X, ZH, Y, CORE), NAMES)
    split = P(NAMES, None)

    return jax.shard_map(
        local, mesh=physical, in_specs=(split, split, split, P()), out_specs=split, check_vma=False
    )
```
